32 devices in a mesh: beam: 8 (over z, x), tile: 4 (over y, core).
Axes of the slice: x: 2, y: 2, z: 4, core: 2. Of those that a mesh axis runs over, the one named last changes fastest.
Arguments:
- atom_counts: bfloat16 [2, 128, 4096], P(None, 'tile'), may hold values from 0 to 4
- beam_index: int32 [8, 2], P('beam'), may hold values from -16 to 16
- beam_weight: float32 [8], P('beam'), may hold values from 0.3 to 3
- probe_rows: int32 [256], P('tile'), may hold values from 0 to 16
- probe_cols: int32 [256], P('tile'), may hold values from 0 to 4095
Outputs:
- intensity: float32 [256, 256], P('tile', 'beam')
The draws below stay inside these ranges and needn't reach their ends.
All inputs are finite; a program needn't handle non-finite values.
Results may differ from the reference program's by a relative error of at most 0.0003.
Values may be sent and summed in bfloat16 or wider, within the bound.
No kernel may reach another device: no remote copies, remote signals or barrier semaphores. Data moves between devices by JAX's collectives and lax.ppermute only.
A program may use at most 64 MiB of HBM per device.

```python
import math
import jax
import jax.numpy as jnp
from jax import lax

BEAM_DEV = 1
ROWS_DEV = 32
NY = 4096
PROBE_DEV = 64
SLICES = 2
CROP = 16
BEAMS = 8
NX = 128
PROBES = 256


def plant(values, own_key, least, largest):
    longest = values.shape.index(max(values.shape))
    spots = []
    for shift in (0, 1):
        where = [jax.random.randint(jax.random.fold_in(own_key, axis), (), 0, length) for axis, length in enumerate(values.shape)]
        where[longest] = (where[longest] + shift) % values.shape[longest]
        spots.append(tuple(where))
    return values.at[spots[0]].set(least).at[spots[1]].set(largest)


def block_scale(rng, dims, pieces, smallest, top_value):
    gain = 1.0
    for position, shards_of in pieces:
        steps = jax.random.uniform(jax.random.fold_in(jax.random.fold_in(rng, 6), position), (shards_of,), jnp.float32, smallest / len(pieces), top_value / len(pieces))
        gain = gain * jnp.repeat(jnp.exp(steps), dims[position] // shards_of).reshape((-1,) + (1,) * (len(dims) - 1 - position))
    return gain


def setup_inputs(seed: int = 0) -> dict:
    splits = jax.random.split(jax.random.key(seed), 6)
    return {
        "atom_counts": jnp.clip(4.0 * jax.random.uniform(splits[0], (SLICES, NX, NY), jnp.float32) ** block_scale(splits[0], (SLICES, NX, NY), ((1, 4),), -0.2, 0.2), 0.0, 4.0).astype(jnp.bfloat16),
        "beam_index": plant(jax.random.randint(splits[1], (BEAMS, 2), -16, 17), jax.random.fold_in(splits[1], 1), -16, 16).astype(jnp.int32),
        "beam_weight": jnp.clip(jnp.exp(math.log(3.0) - 2.3025851 * jax.random.uniform(splits[2], (BEAMS,), jnp.float32) ** block_scale(splits[2], (BEAMS,), ((0, 8),), -0.2, 0.2)), 0.3, 3.0),
        "probe_rows": plant(jax.random.randint(splits[3], (PROBES,), 0, ROWS_DEV - CROP + 1), jax.random.fold_in(splits[3], 1), 0, ROWS_DEV - CROP).astype(jnp.int32),
        "probe_cols": plant(jax.random.randint(splits[4], (PROBES,), 0, NY), jax.random.fold_in(splits[4], 1), 0, NY - 1).astype(jnp.int32),
    }


def make_taps():
    blur_raw = [math.exp(-(offset_index - 5) ** 2 / 4.5) for offset_index in range(11)]
    blur_total = sum(blur_raw)
    spread_raw = [math.exp(-(offset_index - 5) ** 2 / 18.0) for offset_index in range(11)]
    spread_total = sum(spread_raw)
    blur_list = [entry_value / blur_total for entry_value in blur_raw]
    cos_list = [spread_raw[offset_index] / spread_total * math.cos(0.35 * (offset_index - 5) ** 2) for offset_index in range(11)]
    sin_list = [spread_raw[offset_index] / spread_total * math.sin(0.35 * (offset_index - 5) ** 2) for offset_index in range(11)]
    return blur_list, cos_list, sin_list


def blur_axis(values, axis_number):
    blur_taps, cos_taps, sin_taps = make_taps()
    result = blur_taps[0] * jnp.roll(values, 5, axis=axis_number)
    for offset_index in range(1, 11):
        result = result + blur_taps[offset_index] * jnp.roll(values, 5 - offset_index, axis=axis_number)
    return result


def spread_axis(real_part, imag_part, axis_number):
    blur_taps, cos_taps, sin_taps = make_taps()
    out_real = jnp.zeros_like(real_part)
    out_imag = jnp.zeros_like(imag_part)
    for offset_index in range(11):
        shift_real = jnp.roll(real_part, 5 - offset_index, axis=axis_number)
        shift_imag = jnp.roll(imag_part, 5 - offset_index, axis=axis_number)
        out_real = out_real + cos_taps[offset_index] * shift_real - sin_taps[offset_index] * shift_imag
        out_imag = out_imag + cos_taps[offset_index] * shift_imag + sin_taps[offset_index] * shift_real
    return out_real, out_imag


def reference(atom_counts, beam_index, beam_weight, probe_rows, probe_cols):
    counts_float = atom_counts.astype(jnp.float32)
    blurred = blur_axis(blur_axis(counts_float, 1), 2)
    cos_trans = jnp.cos(0.6 * blurred)
    sin_trans = jnp.sin(0.6 * blurred)
    row_grid = jnp.arange(NX, dtype=jnp.int32)
    col_grid = jnp.arange(NY, dtype=jnp.int32)
    probe_total = probe_rows.shape[0]
    global_rows = (jnp.arange(probe_total, dtype=jnp.int32) // PROBE_DEV) * ROWS_DEV + probe_rows
    crop_rows = global_rows[:, None] + jnp.arange(CROP, dtype=jnp.int32)[None, :]
    crop_cols = (probe_cols[:, None] + jnp.arange(CROP, dtype=jnp.int32)[None, :]) % NY

    def one_block(block):
        indices, weights = block
        row_phase = ((indices[:, 0:1] * row_grid[None, :]) % NX).astype(jnp.float32) / NX
        col_phase = ((indices[:, 1:2] * col_grid[None, :]) % NY).astype(jnp.float32) / NY
        angle_grid = 2.0 * math.pi * (row_phase[:, :, None] + col_phase[:, None, :])
        real_part = jnp.cos(angle_grid)
        imag_part = jnp.sin(angle_grid)
        for slice_index in range(SLICES):
            cos_now = cos_trans[slice_index]
            sin_now = sin_trans[slice_index]
            real_part, imag_part = real_part * cos_now - imag_part * sin_now, real_part * sin_now + imag_part * cos_now
            real_part, imag_part = spread_axis(real_part, imag_part, 1)
            real_part, imag_part = spread_axis(real_part, imag_part, 2)
        crop_real = real_part[:, crop_rows[:, :, None], crop_cols[:, None, :]]
        crop_imag = imag_part[:, crop_rows[:, :, None], crop_cols[:, None, :]]
        probe_phase = 2.0 * math.pi * (((indices[:, 0:1] * global_rows[None, :]) % NX).astype(jnp.float32) / NX + ((indices[:, 1:2] * probe_cols[None, :]) % NY).astype(jnp.float32) / NY)
        coef_real = weights[:, None] * jnp.cos(probe_phase)
        coef_imag = -weights[:, None] * jnp.sin(probe_phase)
        exit_real = jnp.einsum("bp,bpuv->puv", coef_real, crop_real) - jnp.einsum("bp,bpuv->puv", coef_imag, crop_imag)
        exit_imag = jnp.einsum("bp,bpuv->puv", coef_real, crop_imag) + jnp.einsum("bp,bpuv->puv", coef_imag, crop_real)
        return exit_real, exit_imag

    blocks = (beam_index.reshape(-1, BEAM_DEV, 2), beam_weight.reshape(-1, BEAM_DEV))
    parts_real, parts_imag = lax.map(one_block, blocks)
    total_real = jnp.sum(parts_real, axis=0)
    total_imag = jnp.sum(parts_imag, axis=0)
    intensity = (total_real * total_real + total_imag * total_imag) / beam_weight.shape[0]
    return intensity.reshape(probe_total, CROP * CROP)
```

```python
import functools
import math

import jax
import jax.numpy as jnp
import numpy as np
from jax import lax
from jax.experimental import pallas as pl
from jax.experimental.pallas import tpu as pltpu
from jax.sharding import PartitionSpec as P

CROP = 16
REACH = 5
LANES = 128
HALF = 64
PAD = 16
PHASE = 0.6
MIDDLE = 1.2


def make_taps():
    blur = [math.exp(-(j * j) / 4.5) for j in range(-REACH, REACH + 1)]
    spread = [math.exp(-(j * j) / 18.0) for j in range(-REACH, REACH + 1)]
    blur = [value / sum(blur) for value in blur]
    spread = [value / sum(spread) for value in spread]
    angles = [0.35 * j * j for j in range(-REACH, REACH + 1)]
    real = [value * math.cos(angle) for value, angle in zip(spread, angles)]
    imag = [value * math.sin(angle) for value, angle in zip(spread, angles)]
    return blur, real, imag


def band(taps, shift=0):
    matrix = np.zeros((HALF, HALF))
    for column in range(HALF):
        for tap, value in enumerate(taps):
            if column + shift + tap < HALF:
                matrix[column + shift + tap, column] = value
    return matrix


def two_parts(matrix):
    high = np.asarray(matrix, np.float32).astype(jnp.bfloat16)
    low = (matrix - high.astype(np.float64)).astype(np.float32).astype(jnp.bfloat16)
    return high, low


def column_matrices():
    blur, real, imag = make_taps()
    real_band, imag_band = band(real), band(imag)
    blurs = []
    for shift in (0, REACH):
        blur_band = band(blur, shift)
        single = np.block([[blur_band, blur_band], [np.zeros((HALF, LANES))]])
        blurs.append(np.concatenate(two_parts(single), axis=0))
    blur_matrix = np.stack(blurs)
    spread = np.block(
        [
            [real_band, imag_band],
            [-imag_band, real_band],
            [-imag_band, real_band],
            [-real_band, -imag_band],
        ]
    )
    spread_high, spread_low = two_parts(spread)
    return blur_matrix, spread_high, spread_low


def fit(function, reach, degree):
    nodes = reach * np.cos(np.pi * (np.arange(200) + 0.5) / 200)
    series = np.polynomial.Chebyshev.fit(nodes, function(nodes), degree, domain=[-reach, reach])
    return series.convert(kind=np.polynomial.Polynomial).coef


def horner(coefficients, value):
    total = coefficients[-1]
    for coefficient in coefficients[-2::-1]:
        total = total * value + coefficient
    return total


def kernel(
    shape,
    rows_ref,
    cols_ref,
    origin_ref,
    main_ref,
    low_ref,
    high_ref,
    beam_ref,
    blur_ref,
    spread_high_ref,
    spread_low_ref,
    out_ref,
    strip,
    patch,
    smooth,
    start_wave,
    parts_high,
    parts_low,
    wave,
):
    grid_rows, grid_cols, beams, take_rows, take_cols = shape
    f32, bf16 = jnp.float32, jnp.bfloat16
    blur, real, imag = make_taps()
    tiles = grid_cols // LANES
    strip_rows = main_ref.shape[1]
    probes = out_ref.shape[0]
    octets = probes // 8
    span = strip_rows + 2 * PAD
    rows_first = take_rows + 6 * REACH
    rows_second = take_rows + 4 * REACH
    load_first = -(-rows_first // 8) * 8
    load_second = -(-rows_second // 8) * 8
    patch_rows = load_first + load_second
    first_row, first_col = origin_ref[0], origin_ref[1]

    def widen(tile, carry):
        lanes = pl.ds(pl.multiple_of(tile * LANES, LANES), LANES)
        for part in range(2):
            base = part * span
            strip[tile, base : base + PAD, :] = low_ref[part, :, lanes].astype(f32)
            strip[tile, base + PAD : base + PAD + strip_rows, :] = main_ref[part, :, lanes].astype(f32)
            strip[tile, base + PAD + strip_rows : base + span, :] = high_ref[part, :, lanes].astype(f32)
        return carry

    lax.fori_loop(0, tiles, widen, 0)

    lane = lax.broadcasted_iota(jnp.int32, (1, LANES), 1)

    def gather(probe, carry):
        row = rows_ref[probe] + first_row + (PAD - 3 * REACH)
        start = lax.rem(cols_ref[probe] + first_col + (grid_cols - 3 * REACH), grid_cols)
        tile = lax.div(start, LANES)
        offset = lax.rem(start, LANES)
        beside = lax.rem(tile + 1, tiles)
        shift = lax.rem(LANES - offset, LANES)
        keep = lane >= offset
        base = pl.multiple_of(probe * patch_rows, 8)
        for at, source, count in (
            (0, row, load_first),
            (load_first, row + span + REACH, load_second),
        ):
            here = strip[tile, pl.ds(source, count), :]
            there = strip[beside, pl.ds(source, count), :]
            moved = pltpu.roll(jnp.where(keep, here, there), shift, 1)
            patch[pl.ds(base + at, count), :] = moved
        return carry

    lax.fori_loop(0, probes, gather, 0, unroll=4)

    group = 8
    for part, source, target, count in (
        (0, 0, 0, rows_first),
        (1, load_first, rows_first, rows_second),
    ):
        for begin in range(0, count, group):
            chosen = range(begin, min(begin + group, count))
            stacked = jnp.concatenate(
                [
                    patch[pl.ds(source + r, probes, stride=patch_rows), :].astype(bf16)
                    for r in chosen
                ],
                axis=0,
            )
            result = jnp.dot(
                jnp.concatenate([stacked, stacked], axis=1),
                blur_ref[part],
                preferred_element_type=f32,
            )
            for at, r in enumerate(chosen):
                smooth[target + r] = result[at * probes : (at + 1) * probes]

    wave_rows = rows_second
    wave_tiles = -(-wave_rows // 8) * 8
    cos_turn = fit(lambda t: np.cos(2 * np.pi * np.sqrt(t + 0.125)), 0.125, 9)
    dx = (
        lax.broadcasted_iota(jnp.int32, (wave_tiles, LANES), 0) + (first_row - 2 * REACH)
    ).astype(f32) / grid_rows
    lanes_full = lax.broadcasted_iota(jnp.int32, (wave_tiles, LANES), 1)
    upper = lanes_full >= HALF
    dy = (
        jnp.where(upper, lanes_full - HALF, lanes_full) + (first_col - 2 * REACH)
    ).astype(f32) / grid_cols
    quarter = jnp.where(upper, 0.25, 0.0).astype(f32)

    def add_beam(beam, total):
        turns = beam_ref[beam, 0:1, :] * dx + beam_ref[beam, 1:2, :] * dy
        turns = turns - jnp.round(turns) - quarter
        turns = turns - jnp.round(turns)
        return total + beam_ref[beam, 2:3, :] * horner(
            [float(c) for c in cos_turn], turns * turns - 0.125
        )

    both = lax.fori_loop(0, beams, add_beam, jnp.zeros((wave_tiles, LANES), f32))
    swapped = pltpu.roll(both, HALF, 1)
    wave_real = jnp.where(upper, swapped, both)
    wave_imag = jnp.where(upper, both, -swapped)
    for r in range(wave_rows):
        start_wave[0, r] = jnp.broadcast_to(wave_real[r : r + 1], (8, LANES))
        start_wave[1, r] = jnp.broadcast_to(wave_imag[r : r + 1], (8, LANES))

    cos_fit = fit(lambda t: np.cos(t + MIDDLE), MIDDLE, 9)
    sin_fit = fit(lambda t: np.sin(t + MIDDLE), MIDDLE, 9)
    lane8 = lax.broadcasted_iota(jnp.int32, (8, LANES), 1)
    wave_fit = [
        jnp.where(lane8 < HALF, float(c), float(s)).astype(f32) for c, s in zip(cos_fit, sin_fit)
    ]
    sign8 = jnp.where(lane8 < HALF, -1.0, 1.0).astype(f32)

    def transmission(window):
        total = (PHASE * blur[REACH]) * window[REACH] - MIDDLE
        for j in range(1, REACH + 1):
            total = total + (PHASE * blur[REACH + j]) * (window[REACH - j] + window[REACH + j])
        return horner(wave_fit, total)

    def split_rows(window):
        real_sum = real[REACH] * window[REACH]
        imag_sum = None
        for j in range(1, REACH + 1):
            pair = window[REACH - j] + window[REACH + j]
            real_sum = real_sum + real[REACH + j] * pair
            term = imag[REACH + j] * pair
            imag_sum = term if imag_sum is None else imag_sum + term
        return real_sum, imag_sum

    def store_parts(slot, value, at, lanes):
        top = value.astype(bf16)
        parts_high[at, slot, lanes] = top.astype(f32)
        parts_low[at, slot, lanes] = value - top.astype(f32)

    def along_columns(count):
        top = parts_high[0:count].reshape(count * probes, 2 * LANES).astype(bf16)
        rest = parts_low[0:count].reshape(count * probes, 2 * LANES).astype(bf16)
        dot = functools.partial(jnp.dot, preferred_element_type=f32)
        return (
            dot(top, spread_high_ref[...])
            + dot(rest, spread_high_ref[...])
            + dot(top, spread_low_ref[...])
        )

    def first_slice(octet, carry):
        slot = pl.ds(pl.multiple_of(octet * 8, 8), 8)
        window, waves = [], []
        for r in range(rows_first):
            window.append(smooth[r, slot, :])
            if r < 2 * REACH:
                continue
            value = transmission(window)
            window.pop(0)
            at = r - 2 * REACH
            waves.append(start_wave[0, at] * value + start_wave[1, at] * pltpu.roll(value, HALF, 1))
            if at < 2 * REACH:
                continue
            real_sum, imag_sum = split_rows(waves)
            waves.pop(0)
            store_parts(slot, real_sum, at - 2 * REACH, slice(0, LANES))
            store_parts(slot, imag_sum, at - 2 * REACH, slice(LANES, 2 * LANES))
        return carry

    lax.fori_loop(0, octets, first_slice, 0)
    middle_rows = take_rows + 2 * REACH
    wave[...] = along_columns(middle_rows).reshape(middle_rows, probes, LANES)

    def second_slice(octet, carry):
        slot = pl.ds(pl.multiple_of(octet * 8, 8), 8)
        window, waves = [], []
        for r in range(rows_second):
            window.append(smooth[rows_first + r, slot, :])
            if r < 2 * REACH:
                continue
            value = transmission(window)
            window.pop(0)
            at = r - 2 * REACH
            now = wave[at, slot, :]
            turned = pltpu.roll(now, HALF, 1)
            now_real = jnp.where(lane8 < HALF, now, turned)
            now_imag = jnp.where(lane8 < HALF, turned, now) * sign8
            waves.append(now_real * value + now_imag * pltpu.roll(value, HALF, 1))
            if at < 2 * REACH:
                continue
            real_sum, imag_sum = split_rows(waves)
            waves.pop(0)
            store_parts(slot, real_sum, at - 2 * REACH, slice(0, LANES))
            store_parts(slot, imag_sum, at - 2 * REACH, slice(LANES, 2 * LANES))
        return carry

    lax.fori_loop(0, octets, second_slice, 0)
    final = along_columns(take_rows)
    power = final * final
    power = (power + pltpu.roll(power, HALF, 1)) * (1.0 / beams)
    lane_all = lax.broadcasted_iota(jnp.int32, (probes, LANES), 1)
    total = power[0:probes]
    for r in range(1, take_rows):
        moved = pltpu.roll(power[r * probes : (r + 1) * probes], r * take_cols, 1)
        total = jnp.where(lane_all >= r * take_cols, moved, total)
    out_ref[...] = total[:, 0 : take_rows * take_cols]


def body(atom_counts, beam_index, beam_weight, probe_rows, probe_cols):
    slices, strip_rows, grid_cols = atom_counts.shape
    beam_parts, tile_parts = lax.axis_size("beam"), lax.axis_size("tile")
    grid_rows = strip_rows * tile_parts
    beams = beam_weight.shape[0] * beam_parts
    probes = probe_rows.shape[0]
    pixels = CROP * CROP // beam_parts
    take_cols = min(pixels, CROP)
    take_rows = pixels // take_cols
    first_pixel = lax.axis_index("beam").astype(jnp.int32) * pixels
    origin = jnp.stack([first_pixel // CROP, first_pixel % CROP])

    forward = [(i, (i + 1) % tile_parts) for i in range(tile_parts)]
    backward = [(target, source) for source, target in forward]
    low = lax.ppermute(atom_counts[:, strip_rows - PAD :], "tile", forward)
    high = lax.ppermute(atom_counts[:, :PAD], "tile", backward)

    numbers = jnp.concatenate([beam_index.astype(jnp.float32), beam_weight[:, None]], axis=1)
    known = jnp.broadcast_to(
        jnp.pad(numbers, ((0, 0), (0, 5)))[:, :, None], (numbers.shape[0], 8, LANES)
    )
    reach = 1
    while reach < beam_parts:
        other = lax.ppermute(known, "beam", [(i, i ^ reach) for i in range(beam_parts)])
        known = jnp.concatenate([known, other], axis=0)
        reach *= 2

    blur_matrix, spread_high, spread_low = column_matrices()
    f32 = jnp.float32
    rows_first = take_rows + 6 * REACH
    rows_second = take_rows + 4 * REACH
    middle_rows = take_rows + 2 * REACH
    patch_rows = -(-rows_first // 8) * 8 + -(-rows_second // 8) * 8
    vmem = pl.BlockSpec(memory_space=pltpu.VMEM)
    smem = pl.BlockSpec(memory_space=pltpu.SMEM)
    call = pl.pallas_call(
        functools.partial(kernel, (grid_rows, grid_cols, beams, take_rows, take_cols)),
        out_shape=jax.ShapeDtypeStruct((probes, pixels), f32),
        in_specs=[smem] * 3 + [vmem] * 7,
        out_specs=vmem,
        scratch_shapes=[
            pltpu.VMEM((grid_cols // LANES, 2 * (strip_rows + 2 * PAD), LANES), f32),
            pltpu.VMEM((probes * patch_rows, LANES), f32),
            pltpu.VMEM((rows_first + rows_second, probes, LANES), f32),
            pltpu.VMEM((2, rows_second, 8, LANES), f32),
            pltpu.VMEM((middle_rows, probes, 2 * LANES), f32),
            pltpu.VMEM((middle_rows, probes, 2 * LANES), f32),
            pltpu.VMEM((middle_rows, probes, LANES), f32),
        ],
        name="window",
    )
    return call(
        probe_rows,
        probe_cols,
        origin,
        atom_counts,
        low,
        high,
        known,
        jnp.asarray(blur_matrix),
        jnp.asarray(spread_high),
        jnp.asarray(spread_low),
    )


def solution(mesh):
    return jax.shard_map(
        body,
        mesh=mesh,
        in_specs=(P(None, "tile", None), P("beam", None), P("beam"), P("tile"), P("tile")),
        out_specs=P("tile", "beam"),
        check_vma=False,
    )
```

```python
import functools
import math

import jax
import jax.numpy as jnp
import numpy as np
from jax import lax
from jax.experimental import pallas as pl
from jax.experimental.pallas import tpu as pltpu
from jax.sharding import PartitionSpec as P


CROP = 16
REACH = 5
LANES = 128
HALF = 64
ROWS = 8
PAD = 16
PHASE = 0.6
MIDDLE = 1.2
NUMBERS = 3


def make_taps():
    blur = [math.exp(-(j * j) / 4.5) for j in range(-REACH, REACH + 1)]
    spread = [math.exp(-(j * j) / 18.0) for j in range(-REACH, REACH + 1)]
    blur = [value / sum(blur) for value in blur]
    spread = [value / sum(spread) for value in spread]
    angles = [0.35 * j * j for j in range(-REACH, REACH + 1)]
    real = [value * math.cos(angle) for value, angle in zip(spread, angles)]
    imag = [value * math.sin(angle) for value, angle in zip(spread, angles)]
    return np.array(blur), np.array(real), np.array(imag)


def two_parts(matrix):
    high = np.asarray(matrix, np.float32).astype(jnp.bfloat16)
    low = (matrix - high.astype(np.float64)).astype(np.float32).astype(jnp.bfloat16)
    return high, low


def band(taps, count):
    matrix = np.zeros((count, count + 2 * REACH))
    for i in range(count):
        matrix[i, i : i + 2 * REACH + 1] = taps
    return matrix


def row_blur(count, stored):
    taps = np.zeros((count, stored))
    taps[:, : count + 2 * REACH] = band(make_taps()[0], count)
    full = np.einsum("rk,pq->rpqk", taps, np.eye(ROWS)).reshape(count * ROWS, ROWS * stored)
    return np.concatenate(two_parts(full), axis=0)


def row_spread(count):
    _, real, imag = make_taps()
    real, imag = band(real, count), band(imag, count)
    taps = np.block([[real, -imag], [imag, real]])
    high, low = two_parts(np.kron(taps, np.eye(ROWS)))
    return np.concatenate([high, high, low], axis=1)


def column_band(taps):
    return np.kron(np.eye(2), np.pad(band(taps, HALF - 2 * REACH), ((0, 2 * REACH), (0, 0))).T)


def column_blur():
    high, low = two_parts(PHASE * column_band(make_taps()[0]))
    return np.block([[high, low], [high, np.zeros_like(low)]])


def column_spread():
    _, real, imag = make_taps()
    real, imag = column_band(real), column_band(imag)
    high, low = two_parts(np.block([[real, imag], [-imag, real]]))
    return np.concatenate([high, high, low], axis=0)


def fit(function, top, degree):
    nodes = top / 2 * (1 + np.cos(np.pi * (np.arange(200) + 0.5) / 200))
    series = np.polynomial.Chebyshev.fit(nodes, function(nodes), degree, domain=[0, top])
    return [float(c) for c in series.convert(kind=np.polynomial.Polynomial).coef]


def horner(coefficients, value):
    total = coefficients[-1]
    for coefficient in coefficients[-2::-1]:
        total = total * value + coefficient
    return total


def split(value):
    high = value.astype(jnp.bfloat16)
    return high, (value - high.astype(jnp.float32)).astype(jnp.bfloat16)


def product(left, right):
    return jnp.dot(left, right, preferred_element_type=jnp.float32)


def column_product(value, matrix):
    high, low = split(value)
    return product(jnp.concatenate([high, low, high], axis=1), matrix)


def row_product(matrix, value):
    high, low = split(value)
    return product(matrix, jnp.concatenate([high, low, high], axis=0))


def transmit(
    plan,
    part,
    rows_ref,
    cols_ref,
    main_ref,
    low_ref,
    high_ref,
    row_matrix,
    column_matrix,
    cos_out,
    sin_out,
    strip,
    patch,
):
    f32 = jnp.float32
    tiles = strip.shape[0]
    grid_cols = tiles * LANES
    strip_rows = main_ref.shape[1]
    halo = (3 - part) * REACH
    stored = patch.shape[0] * 2 // plan.probes
    first_row, first_col = plan.origin()

    def widen(tile, carry):
        lanes = pl.ds(pl.multiple_of(tile * LANES, LANES), LANES)
        strip[tile, 0:PAD, :] = low_ref[:, lanes].astype(f32)
        strip[tile, PAD : PAD + strip_rows, :] = main_ref[part, :, lanes].astype(f32)
        strip[tile, PAD + strip_rows :, :] = high_ref[:, lanes].astype(f32)
        return carry

    lax.fori_loop(0, tiles, widen, 0, unroll=4)
    lane = lax.broadcasted_iota(jnp.int32, (1, LANES), 1)

    def window(probe, place):
        row = rows_ref[probe] + (first_row + (PAD - halo))
        start = cols_ref[probe] + (first_col + (grid_cols - halo))
        start = jnp.where(start >= grid_cols, start - grid_cols, start)
        tile = lax.shift_right_logical(start, 7)
        offset = start & (LANES - 1)
        beside = jnp.where(tile == tiles - 1, 0, tile + 1)
        here = strip[tile, pl.ds(row, stored), :]
        there = strip[beside, pl.ds(row, stored), :]
        shift = (place + LANES - offset) & (LANES - 1)
        return pltpu.roll(jnp.where(lane >= offset, here, there), shift, 1)

    def gather(pair, carry):
        probe = lax.shift_right_logical(pair, 3) * (2 * ROWS) + (pair & (ROWS - 1))
        both = jnp.where(lane < HALF, window(probe, 0), window(probe + ROWS, HALF))
        at = pl.ds(pl.multiple_of(pair * stored, ROWS), stored)
        patch[at, :] = both.astype(patch.dtype)
        return carry

    lax.fori_loop(0, plan.probes // 2, gather, 0, unroll=8)

    cos_fit = fit(lambda t: np.cos(np.sqrt(t)), MIDDLE**2, 4)
    sin_fit = fit(lambda t: np.sinc(np.sqrt(t) / np.pi), MIDDLE**2, 4)
    count = ROWS * stored
    along = []
    for group in range(0, plan.groups, 2):
        counts = [patch[g * count : (g + 1) * count] for g in (group, group + 1)]
        counts = jnp.concatenate([value.astype(jnp.bfloat16) for value in counts], axis=1)
        both = product(row_matrix[...], counts)
        half = both.shape[0] // 2
        both = both[:half] + both[half:]
        along += [both[:, :LANES], both[:, LANES:]]
    phase = product(
        jnp.concatenate(split(jnp.concatenate(along, axis=0)), axis=1), column_matrix[...]
    )
    phase = phase[:, :LANES] + (phase[:, LANES:] - MIDDLE)
    square = phase * phase
    cos_out[...] = horner(cos_fit, square)
    sin_out[...] = phase * horner(sin_fit, square)


def common_wave(plan, beam_ref, wave_ref):
    f32 = jnp.float32
    count = wave_ref.shape[1] // ROWS
    shape = (-(-count // ROWS) * ROWS, LANES)
    beams = beam_ref[...]
    turn_fit = fit(lambda t: np.cos(2 * np.pi * np.sqrt(t)), 0.25, 9)
    first_row, first_col = plan.origin()
    dx = lax.broadcasted_iota(jnp.int32, shape, 0) + (first_row - 2 * REACH)
    lane = lax.broadcasted_iota(jnp.int32, shape, 1)
    upper = lane >= HALF
    dy = (lane & (HALF - 1)) + (first_col - 2 * REACH)
    dx = dx.astype(f32) * (1.0 / plan.grid_rows)
    dy = dy.astype(f32) * (1.0 / plan.grid_cols)
    quarter = jnp.where(upper, 0.25, 0.0).astype(f32)

    both = jnp.zeros(shape, f32)
    for beam in range(plan.beams):
        row, col, weight = [beams[beam : beam + 1, i : i + 1] for i in range(NUMBERS)]
        turns = row * dx + col * dy
        turns = turns - jnp.round(turns) - quarter
        turns = turns - jnp.round(turns)
        both = both + weight * horner(turn_fit, turns * turns)
    turned = pltpu.roll(both, HALF, 1)
    real = jnp.where(upper, turned, both)
    imag = jnp.where(upper, both, turned)
    for r in range(count):
        at = slice(r * ROWS, (r + 1) * ROWS)
        wave_ref[0, at, :] = jnp.broadcast_to(real[r : r + 1], (ROWS, LANES))
        wave_ref[1, at, :] = jnp.broadcast_to(imag[r : r + 1], (ROWS, LANES))


def propagate(waves, row_matrix, column_matrix):
    rows = []
    for i in range(0, len(waves), 2):
        both = row_product(row_matrix[...], jnp.concatenate(waves[i : i + 2], axis=1))
        half = both.shape[0] // 2
        for lanes in (slice(0, LANES), slice(LANES, 2 * LANES)):
            rows.append(jnp.concatenate([both[:half, lanes], both[half:, lanes]], axis=1))
    return column_product(jnp.concatenate(rows, axis=0), column_matrix[...])


def turn(real, imag, cos, sin):
    return jnp.concatenate([real * cos - imag * sin, real * sin + imag * cos], axis=0)


class Plan:
    def __init__(self, grid_rows, grid_cols, beams, probes, pixels):
        self.grid_rows, self.grid_cols = grid_rows, grid_cols
        self.beams, self.probes, self.pixels = beams, probes, pixels
        self.groups = probes // (2 * ROWS)
        self.take_cols = min(pixels, CROP)
        self.take_rows = pixels // self.take_cols
        self.phase_rows = [self.take_rows + 4 * REACH, self.take_rows + 2 * REACH]
        self.stored = [-(-(count + 2 * REACH) // ROWS) * ROWS for count in self.phase_rows]

    def origin(self):
        first = lax.axis_index("beam").astype(jnp.int32) * self.pixels
        return first // CROP, first % CROP


def finish(
    plan,
    beam_ref,
    cos_0,
    sin_0,
    cos_1,
    sin_1,
    spread_rows_0,
    spread_rows_1,
    spread_cols,
    out_ref,
    start,
):
    common_wave(plan, beam_ref, start)
    count = plan.phase_rows[0] * ROWS
    waves = []
    for group in range(plan.groups):
        at = slice(group * count, (group + 1) * count)
        waves.append(turn(start[0], start[1], cos_0[at], sin_0[at]))
    wave = propagate(waves, spread_rows_0, spread_cols)
    count = plan.phase_rows[1] * ROWS
    waves = []
    for group in range(plan.groups):
        at = slice(group * count, (group + 1) * count)
        waves.append(turn(wave[at, :LANES], wave[at, LANES:], cos_1[at], sin_1[at]))
    wave = propagate(waves, spread_rows_1, spread_cols)
    lane = lax.broadcasted_iota(jnp.int32, (ROWS, LANES), 1)
    blocks = []
    count = plan.take_rows * ROWS
    for group in range(plan.groups):
        final = wave[group * count : (group + 1) * count]
        real, imag = final[:, :LANES], final[:, LANES:]
        power = (real * real + imag * imag) * (1.0 / plan.beams)
        for place in (0, HALF):
            block = None
            for r in range(plan.take_rows):
                moved = power[r * ROWS : (r + 1) * ROWS]
                shift = (r * plan.take_cols - place) % LANES
                moved = pltpu.roll(moved, shift, 1) if shift else moved
                block = moved if r == 0 else jnp.where(lane < r * plan.take_cols, block, moved)
            blocks.append(block)
    out_ref[...] = jnp.concatenate(blocks, axis=0).T[: plan.pixels]


def window(atom_counts, beam_index, beam_weight, probe_rows, probe_cols):
    _, strip_rows, grid_cols = atom_counts.shape
    beam_parts, tile_parts = lax.axis_size("beam"), lax.axis_size("tile")
    plan = Plan(
        strip_rows * tile_parts,
        grid_cols,
        beam_weight.shape[0] * beam_parts,
        probe_rows.shape[0],
        CROP * CROP // beam_parts,
    )

    forward = [(i, (i + 1) % tile_parts) for i in range(tile_parts)]
    backward = [(target, source) for source, target in forward]
    known = jnp.concatenate([beam_index.astype(jnp.float32), beam_weight[:, None]], axis=1)
    known = jnp.pad(known, ((0, 0), (0, LANES - NUMBERS)))
    edges = [
        (atom_counts[part, strip_rows - PAD :], atom_counts[part, :PAD]) for part in range(2)
    ]
    known, edges = lax.optimization_barrier((known, edges))

    def share(known, reach):
        other = lax.ppermute(known, "beam", [(i, i ^ reach) for i in range(beam_parts)])
        return jnp.concatenate([known, other], axis=0)

    halos = []
    for part in range(2):
        low = lax.ppermute(edges[part][0], "tile", forward)
        high = lax.ppermute(edges[part][1], "tile", backward)
        halos.append((low, high))
    reach = 1
    while reach < beam_parts:
        known = share(known, reach)
        reach *= 2

    f32, bf16 = jnp.float32, jnp.bfloat16
    vmem = pl.BlockSpec(memory_space=pltpu.VMEM)
    smem = pl.BlockSpec(memory_space=pltpu.SMEM)
    phases = [(plan.groups * count * ROWS, LANES) for count in plan.phase_rows]
    columns = jnp.asarray(column_blur())

    def phase_call(part):
        stored = plan.stored[part]
        low, high = halos[part]
        shape = jax.ShapeDtypeStruct(phases[part], f32)
        kind = bf16 if stored % (2 * ROWS) == 0 else f32
        call = pl.pallas_call(
            functools.partial(transmit, plan, part),
            out_shape=[shape, shape],
            in_specs=[smem] * 2 + [vmem] * 5,
            out_specs=[vmem] * 2,
            scratch_shapes=[
                pltpu.VMEM((grid_cols // LANES, strip_rows + 2 * PAD, LANES), f32),
                pltpu.VMEM((plan.probes // 2 * stored, LANES), kind),
            ],
            compiler_params=pltpu.CompilerParams(vmem_limit_bytes=12 << 20),
        )
        matrix = jnp.asarray(row_blur(plan.phase_rows[part], stored))
        return call(probe_rows, probe_cols, atom_counts, low, high, matrix, columns)

    cos_1, sin_1 = phase_call(1)
    cos_0, sin_0 = phase_call(0)
    call = pl.pallas_call(
        functools.partial(finish, plan),
        out_shape=jax.ShapeDtypeStruct((plan.pixels, plan.probes), f32),
        in_specs=[vmem] * 8,
        out_specs=vmem,
        scratch_shapes=[pltpu.VMEM((2, plan.phase_rows[0] * ROWS, LANES), f32)],
        compiler_params=pltpu.CompilerParams(vmem_limit_bytes=12 << 20),
        name="finish",
    )
    matrices = [
        row_spread(plan.phase_rows[1]),
        row_spread(plan.take_rows),
        column_spread(),
    ]
    out = call(known, cos_0, sin_0, cos_1, sin_1, *[jnp.asarray(m) for m in matrices])
    return out.T


def solution(mesh):
    return jax.shard_map(
        window,
        mesh=mesh,
        in_specs=(P(None, "tile", None), P("beam", None), P("beam"), P("tile"), P("tile")),
        out_specs=P("tile", "beam"),
        check_vma=False,
    )
```

```python
import functools
import math

import jax
import jax.numpy as jnp
import numpy as np
from jax import lax
from jax.experimental import pallas as pl
from jax.experimental.pallas import tpu as pltpu
from jax.sharding import PartitionSpec as P


CROP = 16
REACH = 5
LANES = 128
HALF = 64
ROWS = 8
PAD = 16
PHASE = 0.6
MIDDLE = 1.2
NUMBERS = 3


def make_taps():
    blur = [math.exp(-(j * j) / 4.5) for j in range(-REACH, REACH + 1)]
    spread = [math.exp(-(j * j) / 18.0) for j in range(-REACH, REACH + 1)]
    blur = [value / sum(blur) for value in blur]
    spread = [value / sum(spread) for value in spread]
    angles = [0.35 * j * j for j in range(-REACH, REACH + 1)]
    real = [value * math.cos(angle) for value, angle in zip(spread, angles)]
    imag = [value * math.sin(angle) for value, angle in zip(spread, angles)]
    return np.array(blur), np.array(real), np.array(imag)


def two_parts(matrix):
    high = np.asarray(matrix, np.float32).astype(jnp.bfloat16)
    low = (matrix - high.astype(np.float64)).astype(np.float32).astype(jnp.bfloat16)
    return high, low


def band(taps, count):
    matrix = np.zeros((count, count + 2 * REACH))
    for i in range(count):
        matrix[i, i : i + 2 * REACH + 1] = taps
    return matrix


def row_blur(count, stored):
    taps = np.zeros((count, stored))
    taps[:, : count + 2 * REACH] = band(make_taps()[0], count)
    full = np.einsum("rk,pq->rpqk", taps, np.eye(ROWS)).reshape(count * ROWS, ROWS * stored)
    return np.concatenate(two_parts(full), axis=0)


def row_spread(count):
    _, real, imag = make_taps()
    real, imag = band(real, count), band(imag, count)
    taps = np.block([[real, -imag], [imag, real]])
    high, low = two_parts(np.kron(taps, np.eye(ROWS)))
    return np.concatenate([high, high, low], axis=1)


def column_band(taps):
    return np.kron(np.eye(2), np.pad(band(taps, HALF - 2 * REACH), ((0, 2 * REACH), (0, 0))).T)


def column_blur():
    high, low = two_parts(PHASE * column_band(make_taps()[0]))
    return np.block([[high, low], [high, np.zeros_like(low)]])


def column_spread():
    _, real, imag = make_taps()
    real, imag = column_band(real), column_band(imag)
    high, low = two_parts(np.block([[real, imag], [-imag, real]]))
    return np.concatenate([high, high, low], axis=0)


def fit(function, top, degree):
    nodes = top / 2 * (1 + np.cos(np.pi * (np.arange(200) + 0.5) / 200))
    series = np.polynomial.Chebyshev.fit(nodes, function(nodes), degree, domain=[0, top])
    return [float(c) for c in series.convert(kind=np.polynomial.Polynomial).coef]


def horner(coefficients, value):
    total = coefficients[-1]
    for coefficient in coefficients[-2::-1]:
        total = total * value + coefficient
    return total


def split(value):
    high = value.astype(jnp.bfloat16)
    return high, (value - high.astype(jnp.float32)).astype(jnp.bfloat16)


def product(left, right):
    return jnp.dot(left, right, preferred_element_type=jnp.float32)


def column_product(value, matrix):
    high, low = split(value)
    return product(jnp.concatenate([high, low, high], axis=1), matrix)


def row_product(matrix, value):
    high, low = split(value)
    return product(matrix, jnp.concatenate([high, low, high], axis=0))


def phases(
    plan,
    place_ref,
    main_ref,
    low_ref,
    high_ref,
    table_ref,
    cos_0,
    sin_0,
    cos_1,
    sin_1,
    strip_0,
    strip_1,
    patch_0,
    patch_1,
):
    f32, bf16 = jnp.float32, jnp.bfloat16
    tiles = plan.grid_cols // LANES
    span = plan.span
    strip_rows = main_ref.shape[1]
    strips, patches = (strip_0, strip_1), (patch_0, patch_1)

    def widen(tile, carry):
        lanes = pl.ds(pl.multiple_of(tile * LANES, LANES), LANES)
        at = tile * span
        for part in range(2):
            strips[part][pl.ds(at, PAD), :] = low_ref[part, :, lanes].astype(f32)
            strips[part][pl.ds(at + PAD, strip_rows), :] = main_ref[part, :, lanes].astype(f32)
            strips[part][pl.ds(at + PAD + strip_rows, PAD), :] = high_ref[part, :, lanes].astype(f32)
        return carry

    lax.fori_loop(0, tiles, widen, 0, unroll=4)
    lane = lax.broadcasted_iota(jnp.int32, (1, LANES), 1)
    cos_fit = fit(lambda t: np.cos(np.sqrt(t)), MIDDLE**2, 4)
    sin_fit = fit(lambda t: np.sinc(np.sqrt(t) / np.pi), MIDDLE**2, 4)
    outs = ((cos_0, sin_0), (cos_1, sin_1))
    tables = []
    at = 0
    for shape in plan.tables:
        tables.append(table_ref[at : at + shape[0], : shape[1]])
        at += shape[0]
    for part in (1, 0):
        strip, patch, stored = strips[part], patches[part], plan.stored[part]

        def window(probe):
            here, there, offset, shift = [place_ref[4 * part + i, probe] for i in range(4)]
            both = jnp.where(
                lane >= offset, strip[pl.ds(here, stored), :], strip[pl.ds(there, stored), :]
            )
            return pltpu.roll(both, shift, 1)

        for pair in range(plan.probes // 2):
            probe = pair // ROWS * 2 * ROWS + pair % ROWS
            both = jnp.where(lane < HALF, window(probe), window(probe + ROWS))
            patch[pair * stored : (pair + 1) * stored, :] = both.astype(patch.dtype)

        count = ROWS * stored
        size = plan.phase_rows[part] * ROWS
        for group in range(0, plan.groups, 2):
            counts = [patch[g * count : (g + 1) * count] for g in (group, group + 1)]
            counts = jnp.concatenate([value.astype(bf16) for value in counts], axis=1)
            both = product(tables[part], counts)
            both = both[:size] + both[size:]
            along = jnp.concatenate([both[:, :LANES], both[:, LANES:]], axis=0)
            phase = product(jnp.concatenate(split(along), axis=1), tables[2])
            phase = phase[:, :LANES] + (phase[:, LANES:] - MIDDLE)
            square = phase * phase
            cos_out, sin_out = outs[part]
            cos_out[group * size : (group + 2) * size] = horner(cos_fit, square)
            sin_out[group * size : (group + 2) * size] = phase * horner(sin_fit, square)


def common_wave(plan, beam_ref, wave_ref):
    f32 = jnp.float32
    count = wave_ref.shape[1] // ROWS
    shape = (-(-count // ROWS) * ROWS, LANES)
    beams = beam_ref[...]
    turn_fit = fit(lambda t: np.cos(2 * np.pi * np.sqrt(t)), 0.25, 9)
    first_row, first_col = plan.origin()
    dx = lax.broadcasted_iota(jnp.int32, shape, 0) + (first_row - 2 * REACH)
    lane = lax.broadcasted_iota(jnp.int32, shape, 1)
    upper = lane >= HALF
    dy = (lane & (HALF - 1)) + (first_col - 2 * REACH)
    dx = dx.astype(f32) * (1.0 / plan.grid_rows)
    dy = dy.astype(f32) * (1.0 / plan.grid_cols)
    quarter = jnp.where(upper, 0.25, 0.0).astype(f32)

    both = jnp.zeros(shape, f32)
    for beam in range(plan.beams):
        row, col, weight = [beams[beam : beam + 1, i : i + 1] for i in range(NUMBERS)]
        turns = row * dx + col * dy
        turns = turns - jnp.round(turns) - quarter
        turns = turns - jnp.round(turns)
        both = both + weight * horner(turn_fit, turns * turns)
    turned = pltpu.roll(both, HALF, 1)
    real = jnp.where(upper, turned, both)
    imag = jnp.where(upper, both, turned)
    for r in range(count):
        at = slice(r * ROWS, (r + 1) * ROWS)
        wave_ref[0, at, :] = jnp.broadcast_to(real[r : r + 1], (ROWS, LANES))
        wave_ref[1, at, :] = jnp.broadcast_to(imag[r : r + 1], (ROWS, LANES))


def propagate(waves, row_matrix, column_matrix):
    rows = []
    for i in range(0, len(waves), 2):
        both = row_product(row_matrix[...], jnp.concatenate(waves[i : i + 2], axis=1))
        half = both.shape[0] // 2
        for lanes in (slice(0, LANES), slice(LANES, 2 * LANES)):
            rows.append(jnp.concatenate([both[:half, lanes], both[half:, lanes]], axis=1))
    return column_product(jnp.concatenate(rows, axis=0), column_matrix[...])


def turn(real, imag, cos, sin):
    return jnp.concatenate([real * cos - imag * sin, real * sin + imag * cos], axis=0)


class Plan:
    def __init__(self, grid_rows, grid_cols, beams, probes, pixels, span):
        self.grid_rows, self.grid_cols = grid_rows, grid_cols
        self.beams, self.probes, self.pixels = beams, probes, pixels
        self.groups = probes // (2 * ROWS)
        self.take_cols = min(pixels, CROP)
        self.take_rows = pixels // self.take_cols
        self.halo = [3 * REACH, 2 * REACH]
        self.span = span
        self.phase_rows = [self.take_rows + 4 * REACH, self.take_rows + 2 * REACH]
        self.stored = [-(-(count + 2 * REACH) // ROWS) * ROWS for count in self.phase_rows]

    def origin(self):
        first = lax.axis_index("beam").astype(jnp.int32) * self.pixels
        return first // CROP, first % CROP


def finish(
    plan,
    beam_ref,
    cos_0,
    sin_0,
    cos_1,
    sin_1,
    spread_rows_0,
    spread_rows_1,
    spread_cols,
    out_ref,
    start,
):
    common_wave(plan, beam_ref, start)
    count = plan.phase_rows[0] * ROWS
    waves = []
    for group in range(plan.groups):
        at = slice(group * count, (group + 1) * count)
        waves.append(turn(start[0], start[1], cos_0[at], sin_0[at]))
    wave = propagate(waves, spread_rows_0, spread_cols)
    count = plan.phase_rows[1] * ROWS
    waves = []
    for group in range(plan.groups):
        at = slice(group * count, (group + 1) * count)
        waves.append(turn(wave[at, :LANES], wave[at, LANES:], cos_1[at], sin_1[at]))
    wave = propagate(waves, spread_rows_1, spread_cols)
    lane = lax.broadcasted_iota(jnp.int32, (ROWS, LANES), 1)
    blocks = []
    count = plan.take_rows * ROWS
    for group in range(plan.groups):
        final = wave[group * count : (group + 1) * count]
        real, imag = final[:, :LANES], final[:, LANES:]
        power = (real * real + imag * imag) * (1.0 / plan.beams)
        for place in (0, HALF):
            block = None
            for r in range(plan.take_rows):
                moved = power[r * ROWS : (r + 1) * ROWS]
                shift = (r * plan.take_cols - place) % LANES
                moved = pltpu.roll(moved, shift, 1) if shift else moved
                block = moved if r == 0 else jnp.where(lane < r * plan.take_cols, block, moved)
            blocks.append(block)
    out_ref[...] = jnp.concatenate(blocks, axis=0).T[: plan.pixels]


def window(atom_counts, beam_index, beam_weight, probe_rows, probe_cols):
    _, strip_rows, grid_cols = atom_counts.shape
    beam_parts, tile_parts = lax.axis_size("beam"), lax.axis_size("tile")
    plan = Plan(
        strip_rows * tile_parts,
        grid_cols,
        beam_weight.shape[0] * beam_parts,
        probe_rows.shape[0],
        CROP * CROP // beam_parts,
        strip_rows + 2 * PAD + 1,
    )

    f32, bf16 = jnp.float32, jnp.bfloat16
    vmem = pl.BlockSpec(memory_space=pltpu.VMEM)
    smem = pl.BlockSpec(memory_space=pltpu.SMEM)
    params = pltpu.CompilerParams(vmem_limit_bytes=12 << 20)
    tiles = grid_cols // LANES
    known = jnp.concatenate([beam_index.astype(f32), beam_weight[:, None]], axis=1)
    known = jnp.pad(known, ((0, 0), (0, LANES - NUMBERS)))

    def share(known, reach):
        other = lax.ppermute(known, "beam", [(i, i ^ reach) for i in range(beam_parts)])
        return jnp.concatenate([known, other], axis=0)

    low = atom_counts[:, strip_rows - PAD :]
    high = atom_counts[:, :PAD]

    forward = [(i, (i + 1) % tile_parts) for i in range(tile_parts)]
    backward = [(target, source) for source, target in forward]
    low = lax.ppermute(low, "tile", forward)
    high = lax.ppermute(high, "tile", backward)
    reach = 1
    while reach < beam_parts:
        known = share(known, reach)
        reach *= 2

    first_row, first_col = plan.origin()
    shape = (8, plan.probes)
    which = lax.broadcasted_iota(jnp.int32, shape, 0)
    halo = jnp.where(which < 4, plan.halo[0], plan.halo[1])
    second = lax.broadcasted_iota(jnp.int32, shape, 1) // ROWS % 2 * HALF
    row = probe_rows + (first_row + PAD - halo)
    col = (probe_cols + (first_col + grid_cols - halo)) % grid_cols
    tile, offset = col // LANES, col % LANES
    beside = jnp.where(tile == tiles - 1, 0, tile + 1)
    places = jnp.where(
        which % 4 < 2,
        jnp.where(which % 4 == 0, tile, beside) * plan.span + row,
        jnp.where(which % 4 == 2, offset, (second + LANES - offset) % LANES),
    )

    shapes = [(plan.groups * count * ROWS, LANES) for count in plan.phase_rows]
    shapes = [jax.ShapeDtypeStruct(shape, f32) for shape in shapes]
    patches = []
    for stored in plan.stored:
        kind = bf16 if stored % (2 * ROWS) == 0 else f32
        patches.append(pltpu.VMEM((plan.probes // 2 * stored, LANES), kind))
    call = pl.pallas_call(
        functools.partial(phases, plan),
        out_shape=[shapes[0], shapes[0], shapes[1], shapes[1]],
        in_specs=[smem] + [vmem] * 4,
        out_specs=[vmem] * 4,
        scratch_shapes=[pltpu.VMEM((tiles * plan.span, LANES), f32)] * 2 + patches,
        compiler_params=params,
        name="phases",
    )
    tables = [row_blur(plan.phase_rows[part], plan.stored[part]) for part in range(2)]
    tables.append(column_blur())
    plan.tables = [table.shape for table in tables]
    width = max(cols for _, cols in plan.tables)
    table = np.concatenate([np.pad(t, ((0, 0), (0, width - t.shape[1]))) for t in tables])
    cos_0, sin_0, cos_1, sin_1 = call(places, atom_counts, low, high, jnp.asarray(table))
    call = pl.pallas_call(
        functools.partial(finish, plan),
        out_shape=jax.ShapeDtypeStruct((plan.pixels, plan.probes), f32),
        in_specs=[vmem] * 8,
        out_specs=vmem,
        scratch_shapes=[pltpu.VMEM((2, plan.phase_rows[0] * ROWS, LANES), f32)],
        compiler_params=params,
        name="finish",
    )
    tables = [row_spread(plan.phase_rows[1]), row_spread(plan.take_rows), column_spread()]
    out = call(known, cos_0, sin_0, cos_1, sin_1, *[jnp.asarray(table) for table in tables])
    return out.T


def solution(mesh):
    return jax.shard_map(
        window,
        mesh=mesh,
        in_specs=(P(None, "tile", None), P("beam", None), P("beam"), P("tile"), P("tile")),
        out_specs=P("tile", "beam"),
        check_vma=False,
    )
```

```python
import functools
import math

import jax
import jax.numpy as jnp
import numpy as np
from jax import lax
from jax.experimental import pallas as pl
from jax.experimental.pallas import tpu as pltpu
from jax.sharding import PartitionSpec as P


CROP = 16
REACH = 5
LANES = 128
HALF = 64
ROWS = 8
PAD = 16
NEAR = 8
PHASE = 0.6
MIDDLE = 1.2
NUMBERS = 3


def make_taps():
    blur = [math.exp(-(j * j) / 4.5) for j in range(-REACH, REACH + 1)]
    spread = [math.exp(-(j * j) / 18.0) for j in range(-REACH, REACH + 1)]
    blur = [value / sum(blur) for value in blur]
    spread = [value / sum(spread) for value in spread]
    angles = [0.35 * j * j for j in range(-REACH, REACH + 1)]
    real = [value * math.cos(angle) for value, angle in zip(spread, angles)]
    imag = [value * math.sin(angle) for value, angle in zip(spread, angles)]
    return np.array(blur), np.array(real), np.array(imag)


def two_parts(matrix):
    high = np.asarray(matrix, np.float32).astype(jnp.bfloat16)
    low = (matrix - high.astype(np.float64)).astype(np.float32).astype(jnp.bfloat16)
    return high, low


def band(taps, count):
    matrix = np.zeros((count, count + 2 * REACH))
    for i in range(count):
        matrix[i, i : i + 2 * REACH + 1] = taps
    return matrix


def row_blur(count, stored):
    taps = np.zeros((count, stored))
    taps[:, : count + 2 * REACH] = band(make_taps()[0], count)
    full = np.einsum("rk,pq->rpqk", taps, np.eye(ROWS)).reshape(count * ROWS, ROWS * stored)
    return np.concatenate(two_parts(full), axis=0)


def row_spread(count):
    _, real, imag = make_taps()
    real, imag = band(real, count), band(imag, count)
    taps = np.block([[real, -imag], [imag, real]])
    return np.concatenate(two_parts(np.kron(taps, np.eye(ROWS))), axis=0)


def column_band(taps):
    return np.kron(np.eye(2), np.pad(band(taps, HALF - 2 * REACH), ((0, 2 * REACH), (0, 0))).T)


def column_blur():
    high, low = two_parts(PHASE * column_band(make_taps()[0]))
    return np.block([[high, low], [high, np.zeros_like(low)]])


def column_spread():
    _, real, imag = make_taps()
    real, imag = column_band(real), column_band(imag)
    return np.concatenate(two_parts(np.block([[real, imag], [-imag, real]])), axis=0)


def fit(function, top, degree):
    nodes = top / 2 * (1 + np.cos(np.pi * (np.arange(200) + 0.5) / 200))
    series = np.polynomial.Chebyshev.fit(nodes, function(nodes), degree, domain=[0, top])
    return [float(c) for c in series.convert(kind=np.polynomial.Polynomial).coef]


def ROUNDS(count):
    reaches = []
    while count > 1:
        count //= 2
        reaches.append(count)
    return reaches[::-1]


def horner(coefficients, value):
    total = coefficients[-1]
    for coefficient in coefficients[-2::-1]:
        total = total * value + coefficient
    return total


def split(value):
    high = value.astype(jnp.bfloat16)
    return high, (value - high.astype(jnp.float32)).astype(jnp.bfloat16)


def product(left, right):
    return jnp.dot(left, right, preferred_element_type=jnp.float32)


def column_product(value, matrix):
    count, half = value.shape[0], matrix.shape[0] // 2
    high, low = split(value)
    both = product(jnp.concatenate([high, low], axis=0), matrix[:half])
    return both[:count] + both[count:] + product(high, matrix[half:])


def row_product(matrix, value):
    half = matrix.shape[0] // 2
    high, low = split(value)
    both = product(matrix, high)
    return both[:half] + both[half:] + product(matrix[:half], low)


def choose(plan, top_ref, bottom_ref, rows_ref, cols_ref, _, far_ref, near_ref, place_ref):
    find_places(plan, rows_ref, cols_ref, place_ref)
    first = lax.axis_index("beam") < lax.axis_size("beam") // 2

    @pl.when(first)
    def _():
        far_ref[...] = bottom_ref[...]
        near_ref[...] = top_ref[:, :NEAR, :]

    @pl.when(jnp.logical_not(first))
    def _():
        far_ref[...] = top_ref[...]
        near_ref[...] = bottom_ref[:, PAD - NEAR :, :]


def find_places(plan, rows_ref, cols_ref, place_ref):
    grid_cols = plan.grid_cols
    first_row, first_col = plan.origin()
    shape = place_ref.shape
    which = lax.broadcasted_iota(jnp.int32, shape, 0)
    halo = jnp.where(which < 4, plan.halo[0], plan.halo[1])
    which = which & 3
    second = (lax.broadcasted_iota(jnp.int32, shape, 1) & ROWS) * (HALF // ROWS)
    row = rows_ref[...] + (first_row + PAD - halo)
    col = cols_ref[...] + (first_col + grid_cols - halo)
    col = jnp.where(col >= grid_cols, col - grid_cols, col)
    tile, offset = lax.shift_right_logical(col, 7), col & (LANES - 1)
    beside = jnp.where(tile == grid_cols // LANES - 1, 0, tile + 1)
    place_ref[...] = jnp.where(
        which < 2,
        jnp.where(which == 0, tile, beside) * plan.span + row,
        jnp.where(which == 2, offset, (second + LANES - offset) & (LANES - 1)),
    )


def phases(
    plan,
    place_ref,
    main_ref,
    far_ref,
    near_ref,
    table_ref,
    cos_0,
    sin_0,
    cos_1,
    sin_1,
    strip_0,
    strip_1,
    patch_0,
    patch_1,
):
    f32, bf16 = jnp.float32, jnp.bfloat16
    tiles = plan.grid_cols // LANES
    span = plan.span
    strip_rows = main_ref.shape[1]
    strips, patches = (strip_0, strip_1), (patch_0, patch_1)
    first = lax.axis_index("beam") < lax.axis_size("beam") // 2
    far_at = jnp.where(first, 0, PAD + strip_rows)
    near_at = jnp.where(first, PAD + strip_rows, PAD - NEAR)

    def widen(tile, carry):
        lanes = pl.ds(pl.multiple_of(tile * LANES, LANES), LANES)
        at = tile * span
        for part in range(2):
            strips[part][pl.ds(at + far_at, PAD), :] = far_ref[part, :, lanes].astype(f32)
            strips[part][pl.ds(at + PAD, strip_rows), :] = main_ref[part, :, lanes].astype(f32)
            strips[part][pl.ds(at + near_at, NEAR), :] = near_ref[part, :, lanes].astype(f32)
        return carry

    lax.fori_loop(0, tiles, widen, 0, unroll=4)
    lane = lax.broadcasted_iota(jnp.int32, (1, LANES), 1)
    cos_fit = fit(lambda t: np.cos(np.sqrt(t)), MIDDLE**2, 4)
    sin_fit = fit(lambda t: np.sinc(np.sqrt(t) / np.pi), MIDDLE**2, 4)
    outs = ((cos_0, sin_0), (cos_1, sin_1))
    tables = []
    at = 0
    for shape in plan.tables:
        tables.append(table_ref[at : at + shape[0], : shape[1]])
        at += shape[0]
    for part in (1, 0):
        strip, patch, stored = strips[part], patches[part], plan.stored[part]

        def window(probe):
            here, there, offset, shift = [place_ref[4 * part + i, probe] for i in range(4)]
            both = jnp.where(
                lane >= offset, strip[pl.ds(here, stored), :], strip[pl.ds(there, stored), :]
            )
            return pltpu.roll(both, shift, 1)

        for pair in range(plan.probes // 2):
            probe = pair // ROWS * 2 * ROWS + pair % ROWS
            both = jnp.where(lane < HALF, window(probe), window(probe + ROWS))
            patch[pair * stored : (pair + 1) * stored, :] = both.astype(patch.dtype)

        count = ROWS * stored
        size = plan.phase_rows[part] * ROWS
        for group in range(0, plan.groups, 2):
            counts = [patch[g * count : (g + 1) * count] for g in (group, group + 1)]
            counts = jnp.concatenate([value.astype(bf16) for value in counts], axis=1)
            both = product(tables[part], counts)
            both = both[:size] + both[size:]
            along = jnp.concatenate([both[:, :LANES], both[:, LANES:]], axis=0)
            phase = product(jnp.concatenate(split(along), axis=1), tables[2])
            phase = phase[:, :LANES] + (phase[:, LANES:] - MIDDLE)
            square = phase * phase
            cos_out, sin_out = outs[part]
            cos_out[group * size : (group + 2) * size] = horner(cos_fit, square)
            sin_out[group * size : (group + 2) * size] = phase * horner(sin_fit, square)


def common_wave(plan, beam_ref, wave_ref):
    f32 = jnp.float32
    count = wave_ref.shape[1] // ROWS
    shape = (-(-count // ROWS) * ROWS, LANES)
    turn_fit = fit(lambda t: 2 * np.pi * np.sinc(2 * np.sqrt(t)), 0.0625, 5)
    first_row, first_col = plan.origin()
    dx = lax.broadcasted_iota(jnp.int32, shape, 0) + (first_row - 2 * REACH)
    lane = lax.broadcasted_iota(jnp.int32, shape, 1)
    upper = lane >= HALF
    dy = (lane & (HALF - 1)) + (first_col - 2 * REACH)
    dx = dx.astype(f32) * (1.0 / plan.grid_rows)
    dy = dy.astype(f32) * (1.0 / plan.grid_cols)
    quarter = jnp.where(upper, 0.25, 0.0).astype(f32)

    numbers = [
        jnp.broadcast_to(beam_ref[:, i : i + 1], (plan.beams, LANES)) for i in range(NUMBERS)
    ]
    both = jnp.zeros(shape, f32)
    for beam in range(plan.beams):
        row, col, weight = [number[beam : beam + 1] for number in numbers]
        turns = row * dx + (col * dy - quarter)
        left = 0.25 - jnp.abs(turns - jnp.round(turns))
        both = both + (weight * left) * horner(turn_fit, left * left)
    turned = pltpu.roll(both, HALF, 1)
    real = jnp.where(upper, turned, both)
    imag = jnp.where(upper, both, turned)
    for r in range(count):
        at = slice(r * ROWS, (r + 1) * ROWS)
        wave_ref[0, at, :] = jnp.broadcast_to(real[r : r + 1], (ROWS, LANES))
        wave_ref[1, at, :] = jnp.broadcast_to(imag[r : r + 1], (ROWS, LANES))


def propagate(waves, row_matrix, column_matrix):
    rows = []
    for i in range(0, len(waves), 2):
        both = row_product(row_matrix[...], jnp.concatenate(waves[i : i + 2], axis=1))
        half = both.shape[0] // 2
        for lanes in (slice(0, LANES), slice(LANES, 2 * LANES)):
            rows.append(jnp.concatenate([both[:half, lanes], both[half:, lanes]], axis=1))
    return column_product(jnp.concatenate(rows, axis=0), column_matrix[...])


def turn(real, imag, cos, sin):
    return jnp.concatenate([real * cos - imag * sin, real * sin + imag * cos], axis=0)


class Plan:
    def __init__(self, grid_rows, grid_cols, beams, probes, pixels, span):
        self.grid_rows, self.grid_cols = grid_rows, grid_cols
        self.beams, self.probes, self.pixels = beams, probes, pixels
        self.groups = probes // (2 * ROWS)
        self.take_cols = min(pixels, CROP)
        self.take_rows = pixels // self.take_cols
        self.halo = [3 * REACH, 2 * REACH]
        self.span = span
        self.phase_rows = [self.take_rows + 4 * REACH, self.take_rows + 2 * REACH]
        self.stored = [-(-(count + 2 * REACH) // ROWS) * ROWS for count in self.phase_rows]

    def origin(self):
        first = lax.axis_index("beam").astype(jnp.int32) * self.pixels
        return first // CROP, first % CROP


def finish(
    plan,
    beam_ref,
    cos_0,
    sin_0,
    cos_1,
    sin_1,
    spread_rows_0,
    spread_rows_1,
    spread_cols,
    out_ref,
    start,
):
    common_wave(plan, beam_ref, start)
    count = plan.phase_rows[0] * ROWS
    waves = []
    for group in range(plan.groups):
        at = slice(group * count, (group + 1) * count)
        waves.append(turn(start[0], start[1], cos_0[at], sin_0[at]))
    wave = propagate(waves, spread_rows_0, spread_cols)
    count = plan.phase_rows[1] * ROWS
    waves = []
    for group in range(plan.groups):
        at = slice(group * count, (group + 1) * count)
        waves.append(turn(wave[at, :LANES], wave[at, LANES:], cos_1[at], sin_1[at]))
    wave = propagate(waves, spread_rows_1, spread_cols)
    lane = lax.broadcasted_iota(jnp.int32, (ROWS, LANES), 1)
    blocks = []
    count = plan.take_rows * ROWS
    for group in range(plan.groups):
        final = wave[group * count : (group + 1) * count]
        real, imag = final[:, :LANES], final[:, LANES:]
        power = (real * real + imag * imag) * (1.0 / plan.beams)
        for place in (0, HALF):
            block = None
            for r in range(plan.take_rows):
                moved = power[r * ROWS : (r + 1) * ROWS]
                shift = (r * plan.take_cols - place) % LANES
                moved = pltpu.roll(moved, shift, 1) if shift else moved
                block = moved if r == 0 else jnp.where(lane < r * plan.take_cols, block, moved)
            blocks.append(block)
    out_ref[...] = jnp.concatenate(blocks, axis=0).T[: plan.pixels]


def window(atom_counts, beam_index, beam_weight, probe_rows, probe_cols):
    slices, strip_rows, grid_cols = atom_counts.shape
    beam_parts, tile_parts = lax.axis_size("beam"), lax.axis_size("tile")
    plan = Plan(
        strip_rows * tile_parts,
        grid_cols,
        beam_weight.shape[0] * beam_parts,
        probe_rows.shape[0],
        CROP * CROP // beam_parts,
        strip_rows + 2 * PAD + 1,
    )

    f32, bf16 = jnp.float32, jnp.bfloat16
    vmem = pl.BlockSpec(memory_space=pltpu.VMEM)
    smem = pl.BlockSpec(memory_space=pltpu.SMEM)
    params = pltpu.CompilerParams(vmem_limit_bytes=12 << 20)
    tiles = grid_cols // LANES
    known = jnp.concatenate([beam_index.astype(f32), beam_weight[:, None]], axis=1)
    known = jnp.pad(known, ((0, 0), (0, LANES - NUMBERS)))

    top, bottom = atom_counts[:, :PAD], atom_counts[:, strip_rows - PAD :]
    tables = [row_blur(plan.phase_rows[part], plan.stored[part]) for part in range(2)]
    tables.append(column_blur())
    plan.tables = [table.shape for table in tables]
    width = max(cols for _, cols in plan.tables)
    table = np.concatenate([np.pad(t, ((0, 0), (0, width - t.shape[1]))) for t in tables])
    table = jnp.asarray(table)
    far, near, places = pl.pallas_call(
        functools.partial(choose, plan),
        out_shape=[
            jax.ShapeDtypeStruct((slices, PAD, grid_cols), bf16),
            jax.ShapeDtypeStruct((slices, NEAR, grid_cols), bf16),
            jax.ShapeDtypeStruct((8, plan.probes), jnp.int32),
        ],
        in_specs=[vmem] * 5,
        out_specs=[vmem] * 3,
        compiler_params=pltpu.CompilerParams(vmem_limit_bytes=2 << 20),
        name="choose",
    )(top, bottom, probe_rows[None], probe_cols[None], table)

    def pass_on(rows, step):
        pairs = []
        for beam in range(beam_parts):
            move = step if beam < beam_parts // 2 else -step
            for tile in range(tile_parts):
                pairs.append((beam * tile_parts + tile, beam * tile_parts + (tile + move) % tile_parts))
        return lax.ppermute(rows, ("beam", "tile"), pairs)

    far = pass_on(far, 1)
    near = pass_on(near, -1)
    for reach in ROUNDS(beam_parts):
        other = lax.ppermute(known, "beam", [(i, i ^ reach) for i in range(beam_parts)])
        known = jnp.concatenate([known, other], axis=0)

    shapes = [(plan.groups * count * ROWS, LANES) for count in plan.phase_rows]
    shapes = [jax.ShapeDtypeStruct(shape, f32) for shape in shapes]
    patches = []
    for stored in plan.stored:
        kind = bf16 if stored % (2 * ROWS) == 0 else f32
        patches.append(pltpu.VMEM((plan.probes // 2 * stored, LANES), kind))
    call = pl.pallas_call(
        functools.partial(phases, plan),
        out_shape=[shapes[0], shapes[0], shapes[1], shapes[1]],
        in_specs=[smem] + [vmem] * 4,
        out_specs=[vmem] * 4,
        scratch_shapes=[pltpu.VMEM((tiles * plan.span, LANES), f32)] * 2 + patches,
        compiler_params=params,
        name="phases",
    )
    cos_0, sin_0, cos_1, sin_1 = call(places, atom_counts, far, near, table)
    call = pl.pallas_call(
        functools.partial(finish, plan),
        out_shape=jax.ShapeDtypeStruct((plan.pixels, plan.probes), f32),
        in_specs=[vmem] * 8,
        out_specs=vmem,
        scratch_shapes=[pltpu.VMEM((2, plan.phase_rows[0] * ROWS, LANES), f32)],
        compiler_params=params,
        name="finish",
    )
    tables = [row_spread(plan.phase_rows[1]), row_spread(plan.take_rows), column_spread()]
    out = call(known, cos_0, sin_0, cos_1, sin_1, *[jnp.asarray(table) for table in tables])
    return out.T


def solution(mesh):
    return jax.shard_map(
        window,
        mesh=mesh,
        in_specs=(P(None, "tile", None), P("beam", None), P("beam"), P("tile"), P("tile")),
        out_specs=P("tile", "beam"),
        check_vma=False,
    )
```

```python
import functools
import math

import jax
import jax.numpy as jnp
import numpy as np
from jax import lax
from jax.experimental import pallas as pl
from jax.experimental.pallas import tpu as pltpu
from jax.sharding import PartitionSpec as P


CROP = 16
REACH = 5
LANES = 128
HALF = 64
ROWS = 8
PAD = 16
NEAR = 8
PHASE = 0.6
MIDDLE = 1.2
NUMBERS = 3


def make_taps():
    blur = [math.exp(-(j * j) / 4.5) for j in range(-REACH, REACH + 1)]
    spread = [math.exp(-(j * j) / 18.0) for j in range(-REACH, REACH + 1)]
    blur = [value / sum(blur) for value in blur]
    spread = [value / sum(spread) for value in spread]
    angles = [0.35 * j * j for j in range(-REACH, REACH + 1)]
    real = [value * math.cos(angle) for value, angle in zip(spread, angles)]
    imag = [value * math.sin(angle) for value, angle in zip(spread, angles)]
    return np.array(blur), np.array(real), np.array(imag)


def two_parts(matrix):
    high = np.asarray(matrix, np.float32).astype(jnp.bfloat16)
    low = (matrix - high.astype(np.float64)).astype(np.float32).astype(jnp.bfloat16)
    return high, low


def band(taps, count):
    matrix = np.zeros((count, count + 2 * REACH))
    for i in range(count):
        matrix[i, i : i + 2 * REACH + 1] = taps
    return matrix


def row_blur(count, stored):
    taps = np.zeros((count, stored))
    taps[:, : count + 2 * REACH] = band(make_taps()[0], count)
    full = np.einsum("rk,pq->rpqk", taps, np.eye(ROWS)).reshape(count * ROWS, ROWS * stored)
    return np.concatenate(two_parts(full), axis=0)


def column_band(taps):
    return np.kron(np.eye(2), np.pad(band(taps, HALF - 2 * REACH), ((0, 2 * REACH), (0, 0))).T)


def column_blur():
    high, low = two_parts(PHASE * column_band(make_taps()[0]))
    return np.block([[high, low], [high, np.zeros_like(low)]])


def column_spread():
    _, real, imag = make_taps()
    real, imag = column_band(real), column_band(imag)
    return np.concatenate(two_parts(np.block([[real, imag], [-imag, real]])), axis=0)


def fit(function, top, degree):
    nodes = top / 2 * (1 + np.cos(np.pi * (np.arange(200) + 0.5) / 200))
    series = np.polynomial.Chebyshev.fit(nodes, function(nodes), degree, domain=[0, top])
    return [float(c) for c in series.convert(kind=np.polynomial.Polynomial).coef]


def ROUNDS(count):
    reaches = []
    while count > 1:
        count //= 2
        reaches.append(count)
    return reaches[::-1]


def horner(coefficients, value):
    total = coefficients[-1]
    for coefficient in coefficients[-2::-1]:
        total = total * value + coefficient
    return total


def split(value):
    high = value.astype(jnp.bfloat16)
    return high, (value - high.astype(jnp.float32)).astype(jnp.bfloat16)


def product(left, right):
    return jnp.dot(left, right, preferred_element_type=jnp.float32)


def column_product(value, matrix):
    count, half = value.shape[0], matrix.shape[0] // 2
    high, low = split(value)
    both = product(jnp.concatenate([high, low], axis=0), matrix[:half])
    return both[:count] + both[count:] + product(high, matrix[half:])


def choose(plan, top_ref, bottom_ref, rows_ref, cols_ref, far_ref, near_ref, place_ref):
    find_places(plan, rows_ref, cols_ref, place_ref)
    first = lax.axis_index("beam") < lax.axis_size("beam") // 2

    @pl.when(first)
    def _():
        far_ref[...] = bottom_ref[...]
        near_ref[...] = top_ref[:, :NEAR, :]

    @pl.when(jnp.logical_not(first))
    def _():
        far_ref[...] = top_ref[...]
        near_ref[...] = bottom_ref[:, PAD - NEAR :, :]


def find_places(plan, rows_ref, cols_ref, place_ref):
    grid_cols = plan.grid_cols
    first_row, first_col = plan.origin()
    shape = place_ref.shape
    which = lax.broadcasted_iota(jnp.int32, shape, 0)
    halo = jnp.where(which < 4, plan.halo[0], plan.halo[1])
    which = which & 3
    second = (lax.broadcasted_iota(jnp.int32, shape, 1) & ROWS) * (HALF // ROWS)
    row = rows_ref[...] + (first_row + PAD - halo)
    col = cols_ref[...] + (first_col + grid_cols - halo)
    col = jnp.where(col >= grid_cols, col - grid_cols, col)
    tile, offset = lax.shift_right_logical(col, 7), col & (LANES - 1)
    beside = jnp.where(tile == grid_cols // LANES - 1, 0, tile + 1)
    place_ref[...] = jnp.where(
        which < 2,
        jnp.where(which == 0, tile, beside) * plan.span + row,
        jnp.where(which == 2, offset, (second + LANES - offset) & (LANES - 1)),
    )


def phases(
    plan,
    place_ref,
    top_ref,
    bottom_ref,
    far_ref,
    near_ref,
    table_ref,
    beam_ref,
    cos_0,
    sin_0,
    cos_1,
    sin_1,
    wave_out,
    strip_0,
    strip_1,
    patch_0,
    patch_1,
):
    f32, bf16 = jnp.float32, jnp.bfloat16
    tiles = plan.grid_cols // LANES
    span = plan.span
    strip_rows = 2 * PAD
    strips, patches = (strip_0, strip_1), (patch_0, patch_1)
    first = lax.axis_index("beam") < lax.axis_size("beam") // 2
    far_at = jnp.where(first, 0, PAD + strip_rows)
    near_at = jnp.where(first, PAD + strip_rows, PAD - NEAR)

    for tile in range(tiles):
        lanes = slice(tile * LANES, (tile + 1) * LANES)
        at = tile * span
        for part in range(2):
            strips[part][at + PAD : at + 2 * PAD, :] = top_ref[part, :, lanes].astype(f32)
            strips[part][at + 2 * PAD : at + 3 * PAD, :] = bottom_ref[part, :, lanes].astype(f32)
            strips[part][pl.ds(at + far_at, PAD), :] = far_ref[part, :, lanes].astype(f32)
            strips[part][pl.ds(at + near_at, NEAR), :] = near_ref[part, :, lanes].astype(f32)

    wave_out[...] = common_wave(plan, beam_ref, None)
    lane = lax.broadcasted_iota(jnp.int32, (1, LANES), 1)
    cos_fit = fit(lambda t: np.cos(np.sqrt(t)), MIDDLE**2, 4)
    sin_fit = fit(lambda t: np.sinc(np.sqrt(t) / np.pi), MIDDLE**2, 4)
    outs = ((cos_0, sin_0), (cos_1, sin_1))
    tables = []
    at = 0
    for shape in plan.tables:
        tables.append(table_ref[at : at + shape[0], : shape[1]])
        at += shape[0]
    for part in (1, 0):
        strip, patch, stored = strips[part], patches[part], plan.stored[part]

        def window(probe):
            here, there, offset, shift = [place_ref[4 * part + i, probe] for i in range(4)]
            both = jnp.where(
                lane >= offset, strip[pl.ds(here, stored), :], strip[pl.ds(there, stored), :]
            )
            return pltpu.roll(both, shift, 1)

        for pair in range(plan.probes // 2):
            probe = pair // ROWS * 2 * ROWS + pair % ROWS
            both = jnp.where(lane < HALF, window(probe), window(probe + ROWS))
            patch[pair * stored : (pair + 1) * stored, :] = both.astype(patch.dtype)

        count = ROWS * stored
        size = plan.phase_rows[part] * ROWS
        for group in range(0, plan.groups, 2):
            counts = [patch[g * count : (g + 1) * count] for g in (group, group + 1)]
            counts = jnp.concatenate([value.astype(bf16) for value in counts], axis=1)
            both = product(tables[part], counts)
            both = both[:size] + both[size:]
            along = jnp.concatenate([both[:, :LANES], both[:, LANES:]], axis=0)
            phase = product(jnp.concatenate(split(along), axis=1), tables[2])
            phase = phase[:, :LANES] + (phase[:, LANES:] - MIDDLE)
            square = phase * phase
            cos_out, sin_out = outs[part]
            cos_out[group * size : (group + 2) * size] = horner(cos_fit, square)
            sin_out[group * size : (group + 2) * size] = phase * horner(sin_fit, square)


def common_wave(plan, beam_ref, total):
    f32 = jnp.float32
    turn_fit = fit(lambda t: 2 * np.pi * np.sinc(2 * np.sqrt(t)), 0.0625, 5)
    first_row, first_col = plan.origin()
    shape = plan.wave_shape
    dx = lax.broadcasted_iota(jnp.int32, shape, 0) + (first_row - 2 * REACH)
    lane = lax.broadcasted_iota(jnp.int32, shape, 1)
    dy = (lane & (HALF - 1)) + (first_col - 2 * REACH)
    dx = dx.astype(f32) * (1.0 / plan.grid_rows)
    dy = dy.astype(f32) * (1.0 / plan.grid_cols)
    quarter = jnp.where(lane >= HALF, 0.25, 0.0).astype(f32)
    beams = beam_ref.shape[0]
    numbers = [jnp.broadcast_to(beam_ref[:, i : i + 1], (beams, LANES)) for i in range(NUMBERS)]
    for beam in range(beams):
        row, col, weight = [number[beam : beam + 1] for number in numbers]
        turns = row * dx + (col * dy - quarter)
        left = 0.25 - jnp.abs(turns - jnp.round(turns))
        term = (weight * left) * horner(turn_fit, left * left)
        total = term if total is None else total + term
    return total


def expand_wave(both, wave_ref):
    upper = lax.broadcasted_iota(jnp.int32, both.shape, 1) >= HALF
    turned = pltpu.roll(both, HALF, 1)
    real = jnp.where(upper, turned, both)
    imag = jnp.where(upper, both, turned)
    for r in range(wave_ref.shape[1] // ROWS):
        at = slice(r * ROWS, (r + 1) * ROWS)
        wave_ref[0, at, :] = jnp.broadcast_to(real[r : r + 1], (ROWS, LANES))
        wave_ref[1, at, :] = jnp.broadcast_to(imag[r : r + 1], (ROWS, LANES))


def spread_rows(wave, count):
    _, real_taps, imag_taps = make_taps()
    half = wave.shape[0] // 2
    out = []
    for at in range(count):
        sums = []
        for base in (0, half):
            rows = [
                wave[base + (at + j) * ROWS : base + (at + j + 1) * ROWS] for j in range(2 * REACH + 1)
            ]
            pairs = [rows[REACH]] + [rows[REACH - j] + rows[REACH + j] for j in range(1, REACH + 1)]
            sums.append(
                [
                    sum(float(taps[REACH + j]) * pairs[j] for j in range(start, REACH + 1))
                    for taps, start in ((real_taps, 0), (imag_taps, 1))
                ]
            )
        (real_real, real_imag), (imag_real, imag_imag) = sums
        out.append(jnp.concatenate([real_real - imag_imag, imag_real + real_imag], axis=1))
    return jnp.concatenate(out, axis=0)


def turn(real, imag, cos, sin):
    return jnp.concatenate([real * cos - imag * sin, real * sin + imag * cos], axis=0)


class Plan:
    def __init__(self, grid_rows, grid_cols, beams, probes, pixels, span):
        self.grid_rows, self.grid_cols = grid_rows, grid_cols
        self.beams, self.probes, self.pixels = beams, probes, pixels
        self.groups = probes // (2 * ROWS)
        self.take_cols = min(pixels, CROP)
        self.take_rows = pixels // self.take_cols
        self.halo = [3 * REACH, 2 * REACH]
        self.span = span
        self.wave_shape = (-(-(self.take_rows + 4 * REACH) // ROWS) * ROWS, LANES)
        self.phase_rows = [self.take_rows + 4 * REACH, self.take_rows + 2 * REACH]
        self.stored = [-(-(count + 2 * REACH) // ROWS) * ROWS for count in self.phase_rows]

    def origin(self):
        first = lax.axis_index("beam").astype(jnp.int32) * self.pixels
        return first // CROP, first % CROP


def finish(
    plan,
    beam_ref,
    half_wave,
    cos_0,
    sin_0,
    cos_1,
    sin_1,
    spread_cols,
    out_ref,
    start,
):
    expand_wave(common_wave(plan, beam_ref, half_wave[...]), start)
    count = plan.phase_rows[0] * ROWS
    waves = []
    for group in range(plan.groups):
        at = slice(group * count, (group + 1) * count)
        waves.append(turn(start[0], start[1], cos_0[at], sin_0[at]))
    rows = [spread_rows(wave, plan.phase_rows[1]) for wave in waves]
    wave = column_product(jnp.concatenate(rows, axis=0), spread_cols[...])
    count = plan.phase_rows[1] * ROWS
    waves = []
    for group in range(plan.groups):
        at = slice(group * count, (group + 1) * count)
        waves.append(turn(wave[at, :LANES], wave[at, LANES:], cos_1[at], sin_1[at]))
    rows = [spread_rows(wave, plan.take_rows) for wave in waves]
    wave = column_product(jnp.concatenate(rows, axis=0), spread_cols[...])
    lane = lax.broadcasted_iota(jnp.int32, (ROWS, LANES), 1)
    blocks = []
    count = plan.take_rows * ROWS
    for group in range(plan.groups):
        final = wave[group * count : (group + 1) * count]
        real, imag = final[:, :LANES], final[:, LANES:]
        power = (real * real + imag * imag) * (1.0 / plan.beams)
        for place in (0, HALF):
            block = None
            for r in range(plan.take_rows):
                moved = power[r * ROWS : (r + 1) * ROWS]
                shift = (r * plan.take_cols - place) % LANES
                moved = pltpu.roll(moved, shift, 1) if shift else moved
                block = moved if r == 0 else jnp.where(lane < r * plan.take_cols, block, moved)
            blocks.append(block)
    out_ref[...] = jnp.concatenate(blocks, axis=0).T[: plan.pixels]


def window(atom_counts, beam_index, beam_weight, probe_rows, probe_cols):
    slices, strip_rows, grid_cols = atom_counts.shape
    beam_parts, tile_parts = lax.axis_size("beam"), lax.axis_size("tile")
    plan = Plan(
        strip_rows * tile_parts,
        grid_cols,
        beam_weight.shape[0] * beam_parts,
        probe_rows.shape[0],
        CROP * CROP // beam_parts,
        strip_rows + 2 * PAD + 1,
    )

    f32, bf16 = jnp.float32, jnp.bfloat16
    vmem = pl.BlockSpec(memory_space=pltpu.VMEM)
    smem = pl.BlockSpec(memory_space=pltpu.SMEM)
    params = pltpu.CompilerParams(vmem_limit_bytes=12 << 20)
    tiles = grid_cols // LANES
    known = jnp.concatenate([beam_index.astype(f32), beam_weight[:, None]], axis=1)
    known = jnp.pad(known, ((0, 0), (0, LANES - NUMBERS)))

    top, bottom = atom_counts[:, :PAD], atom_counts[:, strip_rows - PAD :]
    tables = [row_blur(plan.phase_rows[part], plan.stored[part]) for part in range(2)]
    tables.append(column_blur())
    plan.tables = [table.shape for table in tables]
    width = max(cols for _, cols in plan.tables)
    table = np.concatenate([np.pad(t, ((0, 0), (0, width - t.shape[1]))) for t in tables])
    table = jnp.asarray(table)
    far, near, places = pl.pallas_call(
        functools.partial(choose, plan),
        out_shape=[
            jax.ShapeDtypeStruct((slices, PAD, grid_cols), bf16),
            jax.ShapeDtypeStruct((slices, NEAR, grid_cols), bf16),
            jax.ShapeDtypeStruct((8, plan.probes), jnp.int32),
        ],
        in_specs=[vmem] * 4,
        out_specs=[vmem] * 3,
        compiler_params=pltpu.CompilerParams(vmem_limit_bytes=2 << 20),
        name="choose",
    )(top, bottom, probe_rows[None], probe_cols[None])

    def pass_on(rows, step):
        pairs = []
        for beam in range(beam_parts):
            move = step if beam < beam_parts // 2 else -step
            for tile in range(tile_parts):
                pairs.append((beam * tile_parts + tile, beam * tile_parts + (tile + move) % tile_parts))
        return lax.ppermute(rows, ("beam", "tile"), pairs)

    far = pass_on(far, 1)
    near = pass_on(near, -1)
    other = None
    for reach in ROUNDS(beam_parts):
        if other is not None:
            known = jnp.concatenate([known, other], axis=0)
        other = lax.ppermute(known, "beam", [(i, i ^ reach) for i in range(beam_parts)])

    shapes = [(plan.groups * count * ROWS, LANES) for count in plan.phase_rows]
    shapes = [jax.ShapeDtypeStruct(shape, f32) for shape in shapes]
    patches = []
    for stored in plan.stored:
        kind = bf16 if stored % (2 * ROWS) == 0 else f32
        patches.append(pltpu.VMEM((plan.probes // 2 * stored, LANES), kind))
    call = pl.pallas_call(
        functools.partial(phases, plan),
        out_shape=[shapes[0]] * 2 + [shapes[1]] * 2 + [jax.ShapeDtypeStruct(plan.wave_shape, f32)],
        in_specs=[smem] + [vmem] * 6,
        out_specs=[vmem] * 5,
        scratch_shapes=[pltpu.VMEM((tiles * plan.span, LANES), f32)] * 2 + patches,
        compiler_params=params,
        name="phases",
    )
    cos_0, sin_0, cos_1, sin_1, wave = call(
        places, top, bottom, far, near, table, known
    )
    call = pl.pallas_call(
        functools.partial(finish, plan),
        out_shape=jax.ShapeDtypeStruct((plan.pixels, plan.probes), f32),
        in_specs=[vmem] * 7,
        out_specs=vmem,
        scratch_shapes=[pltpu.VMEM((2, plan.phase_rows[0] * ROWS, LANES), f32)],
        compiler_params=params,
        name="finish",
    )
    out = call(other, wave, cos_0, sin_0, cos_1, sin_1, jnp.asarray(column_spread()))
    return out.T


def solution(mesh):
    return jax.shard_map(
        window,
        mesh=mesh,
        in_specs=(P(None, "tile", None), P("beam", None), P("beam"), P("tile"), P("tile")),
        out_specs=P("tile", "beam"),
        check_vma=False,
    )
```

```python
import functools
import math

import jax
import jax.numpy as jnp
import numpy as np
from jax import lax
from jax.experimental import pallas as pl
from jax.experimental.pallas import tpu as pltpu
from jax.sharding import PartitionSpec as P


CROP = 16
REACH = 5
LANES = 128
HALF = 64
ROWS = 8
PAD = 16
NEAR = 8
PHASE = 0.6
MIDDLE = 1.2
NUMBERS = 3


def make_taps():
    blur = [math.exp(-(j * j) / 4.5) for j in range(-REACH, REACH + 1)]
    spread = [math.exp(-(j * j) / 18.0) for j in range(-REACH, REACH + 1)]
    blur = [value / sum(blur) for value in blur]
    spread = [value / sum(spread) for value in spread]
    angles = [0.35 * j * j for j in range(-REACH, REACH + 1)]
    real = [value * math.cos(angle) for value, angle in zip(spread, angles)]
    imag = [value * math.sin(angle) for value, angle in zip(spread, angles)]
    return np.array(blur), np.array(real), np.array(imag)


def two_parts(matrix):
    high = np.asarray(matrix, np.float32).astype(jnp.bfloat16)
    low = (matrix - high.astype(np.float64)).astype(np.float32).astype(jnp.bfloat16)
    return high, low


def band(taps, count):
    matrix = np.zeros((count, count + 2 * REACH))
    for i in range(count):
        matrix[i, i : i + 2 * REACH + 1] = taps
    return matrix


def row_blur(count, stored):
    taps = np.zeros((count, stored))
    taps[:, : count + 2 * REACH] = band(make_taps()[0], count)
    full = np.einsum("rk,pq->rpqk", taps, np.eye(ROWS)).reshape(count * ROWS, ROWS * stored)
    return np.concatenate(two_parts(full), axis=0)


def column_band(taps):
    return np.kron(np.eye(2), np.pad(band(taps, HALF - 2 * REACH), ((0, 2 * REACH), (0, 0))).T)


def column_blur():
    high, low = two_parts(PHASE * column_band(make_taps()[0]))
    return np.block([[high, low], [high, np.zeros_like(low)]])


def column_spread():
    _, real, imag = make_taps()
    real, imag = column_band(real), column_band(imag)
    return np.concatenate(two_parts(np.block([[real, imag], [-imag, real]])), axis=0)


def fit(function, top, degree):
    nodes = top / 2 * (1 + np.cos(np.pi * (np.arange(200) + 0.5) / 200))
    series = np.polynomial.Chebyshev.fit(nodes, function(nodes), degree, domain=[0, top])
    return [float(c) for c in series.convert(kind=np.polynomial.Polynomial).coef]


def ROUNDS(count):
    reaches = []
    while count > 1:
        count //= 2
        reaches.append(count)
    return reaches[::-1]


def horner(coefficients, value):
    total = coefficients[-1]
    for coefficient in coefficients[-2::-1]:
        total = total * value + coefficient
    return total


def split(value):
    high = value.astype(jnp.bfloat16)
    return high, (value - high.astype(jnp.float32)).astype(jnp.bfloat16)


def product(left, right):
    return jnp.dot(left, right, preferred_element_type=jnp.float32)


def column_product(value, matrix):
    count, half = value.shape[0], matrix.shape[0] // 2
    high, low = split(value)
    both = product(jnp.concatenate([high, low], axis=0), matrix[:half])
    return both[:count] + both[count:] + product(high, matrix[half:])


def choose(plan, top_ref, bottom_ref, rows_ref, cols_ref, far_ref, near_ref, place_ref):
    find_places(plan, rows_ref, cols_ref, place_ref)
    first = lax.axis_index("beam") < lax.axis_size("beam") // 2

    @pl.when(first)
    def _():
        far_ref[...] = bottom_ref[...]
        near_ref[...] = top_ref[:, :NEAR, :]

    @pl.when(jnp.logical_not(first))
    def _():
        far_ref[...] = top_ref[...]
        near_ref[...] = bottom_ref[:, PAD - NEAR :, :]


def find_places(plan, rows_ref, cols_ref, place_ref):
    grid_cols = plan.grid_cols
    first_row, first_col = plan.origin()
    shape = place_ref.shape
    which = lax.broadcasted_iota(jnp.int32, shape, 0)
    halo = jnp.where(which < 4, plan.halo[0], plan.halo[1])
    which = which & 3
    second = (lax.broadcasted_iota(jnp.int32, shape, 1) & ROWS) * (HALF // ROWS)
    row = rows_ref[...] + (first_row + PAD - halo)
    col = cols_ref[...] + (first_col + grid_cols - halo)
    col = jnp.where(col >= grid_cols, col - grid_cols, col)
    tile, offset = lax.shift_right_logical(col, 7), col & (LANES - 1)
    beside = jnp.where(tile == grid_cols // LANES - 1, 0, tile + 1)
    place_ref[...] = jnp.where(
        which < 2,
        jnp.where(which == 0, tile, beside) * plan.span + row,
        jnp.where(which == 2, offset, (second + LANES - offset) & (LANES - 1)),
    )


def phases(
    plan,
    found_ref,
    top_ref,
    bottom_ref,
    far_ref,
    near_ref,
    table_ref,
    beam_ref,
    cos_0,
    sin_0,
    cos_1,
    sin_1,
    wave_out,
    strip_0,
    strip_1,
    patch_0,
    patch_1,
    place_ref,
    arrived,
):
    f32, bf16 = jnp.float32, jnp.bfloat16
    tiles = plan.grid_cols // LANES
    span = plan.span
    strip_rows = 2 * PAD
    strips, patches = (strip_0, strip_1), (patch_0, patch_1)
    transfer = pltpu.make_async_copy(found_ref, place_ref, arrived)
    transfer.start()
    first = lax.axis_index("beam") < lax.axis_size("beam") // 2
    far_at = jnp.where(first, 0, PAD + strip_rows)
    near_at = jnp.where(first, PAD + strip_rows, PAD - NEAR)

    for tile in range(tiles):
        lanes = slice(tile * LANES, (tile + 1) * LANES)
        at = tile * span
        for part in range(2):
            strips[part][at + PAD : at + 2 * PAD, :] = top_ref[part, :, lanes].astype(f32)
            strips[part][at + 2 * PAD : at + 3 * PAD, :] = bottom_ref[part, :, lanes].astype(f32)
            strips[part][pl.ds(at + far_at, PAD), :] = far_ref[part, :, lanes].astype(f32)
            strips[part][pl.ds(at + near_at, NEAR), :] = near_ref[part, :, lanes].astype(f32)

    wave_out[...] = common_wave(plan, beam_ref, None)
    transfer.wait()
    lane = lax.broadcasted_iota(jnp.int32, (1, LANES), 1)
    lower = jnp.where(lane < HALF, 1.0, 0.0).astype(bf16)
    upper = jnp.where(lane < HALF, 0.0, 1.0).astype(bf16)
    cos_fit = fit(lambda t: np.cos(np.sqrt(t)), MIDDLE**2, 4)
    sin_fit = fit(lambda t: np.sinc(np.sqrt(t) / np.pi), MIDDLE**2, 4)
    outs = ((cos_0, sin_0), (cos_1, sin_1))
    tables = []
    at = 0
    for shape in plan.tables:
        tables.append(table_ref[at : at + shape[0], : shape[1]])
        at += shape[0]
    for part in (1, 0):
        strip, patch, stored = strips[part], patches[part], plan.stored[part]

        def window(probe):
            here, there, offset, shift = [place_ref[4 * part + i, probe] for i in range(4)]
            both = jnp.where(
                lane >= offset, strip[pl.ds(here, stored), :], strip[pl.ds(there, stored), :]
            )
            return pltpu.roll(both, shift, 1)

        for pair in range(plan.probes // 2):
            probe = pair // ROWS * 2 * ROWS + pair % ROWS
            both = lower * window(probe).astype(bf16) + upper * window(probe + ROWS).astype(bf16)
            patch[pair * stored : (pair + 1) * stored, :] = both.astype(patch.dtype)

        count = ROWS * stored
        size = plan.phase_rows[part] * ROWS
        for group in range(0, plan.groups, 2):
            counts = [patch[g * count : (g + 1) * count] for g in (group, group + 1)]
            counts = jnp.concatenate([value.astype(bf16) for value in counts], axis=1)
            both = product(tables[part], counts)
            both = both[:size] + both[size:]
            along = jnp.concatenate([both[:, :LANES], both[:, LANES:]], axis=0)
            phase = product(jnp.concatenate(split(along), axis=1), tables[2])
            phase = phase[:, :LANES] + (phase[:, LANES:] - MIDDLE)
            square = phase * phase
            cos_out, sin_out = outs[part]
            cos_out[group * size : (group + 2) * size] = horner(cos_fit, square)
            sin_out[group * size : (group + 2) * size] = phase * horner(sin_fit, square)


def common_wave(plan, beam_ref, total):
    f32 = jnp.float32
    turn_fit = fit(lambda t: 2 * np.pi * np.sinc(2 * np.sqrt(t)), 0.0625, 5)
    first_row, first_col = plan.origin()
    shape = plan.wave_shape
    dx = lax.broadcasted_iota(jnp.int32, shape, 0) + (first_row - 2 * REACH)
    lane = lax.broadcasted_iota(jnp.int32, shape, 1)
    dy = (lane & (HALF - 1)) + (first_col - 2 * REACH)
    dx = dx.astype(f32) * (1.0 / plan.grid_rows)
    dy = dy.astype(f32) * (1.0 / plan.grid_cols)
    quarter = jnp.where(lane >= HALF, 0.25, 0.0).astype(f32)
    beams = beam_ref.shape[0]
    numbers = [jnp.broadcast_to(beam_ref[:, i : i + 1], (beams, LANES)) for i in range(NUMBERS)]
    for beam in range(beams):
        row, col, weight = [number[beam : beam + 1] for number in numbers]
        turns = row * dx + (col * dy - quarter)
        left = 0.25 - jnp.abs(turns - jnp.round(turns))
        term = (weight * left) * horner(turn_fit, left * left)
        total = term if total is None else total + term
    return total


def expand_wave(both, wave_ref):
    upper = lax.broadcasted_iota(jnp.int32, both.shape, 1) >= HALF
    turned = pltpu.roll(both, HALF, 1)
    real = jnp.where(upper, turned, both)
    imag = jnp.where(upper, both, turned)
    for r in range(wave_ref.shape[1] // ROWS):
        at = slice(r * ROWS, (r + 1) * ROWS)
        wave_ref[0, at, :] = jnp.broadcast_to(real[r : r + 1], (ROWS, LANES))
        wave_ref[1, at, :] = jnp.broadcast_to(imag[r : r + 1], (ROWS, LANES))


def spread_rows(wave, count):
    _, real_taps, imag_taps = make_taps()
    half = wave.shape[0] // 2
    out = []
    for at in range(count):
        sums = []
        for base in (0, half):
            rows = [
                wave[base + (at + j) * ROWS : base + (at + j + 1) * ROWS] for j in range(2 * REACH + 1)
            ]
            pairs = [rows[REACH]] + [rows[REACH - j] + rows[REACH + j] for j in range(1, REACH + 1)]
            sums.append(
                [
                    sum(float(taps[REACH + j]) * pairs[j] for j in range(start, REACH + 1))
                    for taps, start in ((real_taps, 0), (imag_taps, 1))
                ]
            )
        (real_real, real_imag), (imag_real, imag_imag) = sums
        out.append(jnp.concatenate([real_real - imag_imag, imag_real + real_imag], axis=1))
    return jnp.concatenate(out, axis=0)


def turn(real, imag, cos, sin):
    return jnp.concatenate([real * cos - imag * sin, real * sin + imag * cos], axis=0)


class Plan:
    def __init__(self, grid_rows, grid_cols, beams, probes, pixels, span):
        self.grid_rows, self.grid_cols = grid_rows, grid_cols
        self.beams, self.probes, self.pixels = beams, probes, pixels
        self.groups = probes // (2 * ROWS)
        self.take_cols = min(pixels, CROP)
        self.take_rows = pixels // self.take_cols
        self.halo = [3 * REACH, 2 * REACH]
        self.span = span
        self.wave_shape = (-(-(self.take_rows + 4 * REACH) // ROWS) * ROWS, LANES)
        self.phase_rows = [self.take_rows + 4 * REACH, self.take_rows + 2 * REACH]
        self.stored = [-(-(count + 2 * REACH) // ROWS) * ROWS for count in self.phase_rows]

    def origin(self):
        first = lax.axis_index("beam").astype(jnp.int32) * self.pixels
        return first // CROP, first % CROP


def finish(
    plan,
    beam_ref,
    half_wave,
    cos_0,
    sin_0,
    cos_1,
    sin_1,
    spread_cols,
    out_ref,
    start,
):
    expand_wave(common_wave(plan, beam_ref, half_wave[...]), start)
    count = plan.phase_rows[0] * ROWS
    waves = []
    for group in range(plan.groups):
        at = slice(group * count, (group + 1) * count)
        waves.append(turn(start[0], start[1], cos_0[at], sin_0[at]))
    rows = [spread_rows(wave, plan.phase_rows[1]) for wave in waves]
    wave = column_product(jnp.concatenate(rows, axis=0), spread_cols[...])
    count = plan.phase_rows[1] * ROWS
    waves = []
    for group in range(plan.groups):
        at = slice(group * count, (group + 1) * count)
        waves.append(turn(wave[at, :LANES], wave[at, LANES:], cos_1[at], sin_1[at]))
    rows = [spread_rows(wave, plan.take_rows) for wave in waves]
    wave = column_product(jnp.concatenate(rows, axis=0), spread_cols[...])
    lane = lax.broadcasted_iota(jnp.int32, (ROWS, LANES), 1)
    blocks = []
    count = plan.take_rows * ROWS
    for group in range(plan.groups):
        final = wave[group * count : (group + 1) * count]
        real, imag = final[:, :LANES], final[:, LANES:]
        power = (real * real + imag * imag) * (1.0 / plan.beams)
        for place in (0, HALF):
            block = None
            for r in range(plan.take_rows):
                moved = power[r * ROWS : (r + 1) * ROWS]
                shift = (r * plan.take_cols - place) % LANES
                moved = pltpu.roll(moved, shift, 1) if shift else moved
                block = moved if r == 0 else jnp.where(lane < r * plan.take_cols, block, moved)
            blocks.append(block)
    out_ref[...] = jnp.concatenate(blocks, axis=0).T[: plan.pixels]


def window(atom_counts, beam_index, beam_weight, probe_rows, probe_cols):
    slices, strip_rows, grid_cols = atom_counts.shape
    beam_parts, tile_parts = lax.axis_size("beam"), lax.axis_size("tile")
    plan = Plan(
        strip_rows * tile_parts,
        grid_cols,
        beam_weight.shape[0] * beam_parts,
        probe_rows.shape[0],
        CROP * CROP // beam_parts,
        strip_rows + 2 * PAD + 1,
    )

    f32, bf16 = jnp.float32, jnp.bfloat16
    vmem = pl.BlockSpec(memory_space=pltpu.VMEM)
    smem = pl.BlockSpec(memory_space=pltpu.SMEM)
    params = pltpu.CompilerParams(vmem_limit_bytes=12 << 20)
    tiles = grid_cols // LANES
    known = jnp.concatenate([beam_index.astype(f32), beam_weight[:, None]], axis=1)
    known = jnp.pad(known, ((0, 0), (0, LANES - NUMBERS)))

    top, bottom = atom_counts[:, :PAD], atom_counts[:, strip_rows - PAD :]
    tables = [row_blur(plan.phase_rows[part], plan.stored[part]) for part in range(2)]
    tables.append(column_blur())
    plan.tables = [table.shape for table in tables]
    width = max(cols for _, cols in plan.tables)
    table = np.concatenate([np.pad(t, ((0, 0), (0, width - t.shape[1]))) for t in tables])
    table = jnp.asarray(table)
    far, near, places = pl.pallas_call(
        functools.partial(choose, plan),
        out_shape=[
            jax.ShapeDtypeStruct((slices, PAD, grid_cols), bf16),
            jax.ShapeDtypeStruct((slices, NEAR, grid_cols), bf16),
            jax.ShapeDtypeStruct((8, plan.probes), jnp.int32),
        ],
        in_specs=[vmem] * 4,
        out_specs=[vmem] * 3,
        compiler_params=pltpu.CompilerParams(vmem_limit_bytes=2 << 20),
        name="choose",
    )(top, bottom, probe_rows[None], probe_cols[None])

    def pass_on(rows, step):
        pairs = []
        for beam in range(beam_parts):
            move = step if beam < beam_parts // 2 else -step
            for tile in range(tile_parts):
                pairs.append((beam * tile_parts + tile, beam * tile_parts + (tile + move) % tile_parts))
        return lax.ppermute(rows, ("beam", "tile"), pairs)

    far = pass_on(far, 1)
    near = pass_on(near, -1)
    other = None
    for reach in ROUNDS(beam_parts):
        if other is not None:
            known = jnp.concatenate([known, other], axis=0)
        other = lax.ppermute(known, "beam", [(i, i ^ reach) for i in range(beam_parts)])

    shapes = [(plan.groups * count * ROWS, LANES) for count in plan.phase_rows]
    shapes = [jax.ShapeDtypeStruct(shape, f32) for shape in shapes]
    patches = []
    for stored in plan.stored:
        kind = bf16 if stored % (2 * ROWS) == 0 else f32
        patches.append(pltpu.VMEM((plan.probes // 2 * stored, LANES), kind))
    call = pl.pallas_call(
        functools.partial(phases, plan),
        out_shape=[shapes[0]] * 2 + [shapes[1]] * 2 + [jax.ShapeDtypeStruct(plan.wave_shape, f32)],
        in_specs=[vmem] * 7,
        out_specs=[vmem] * 5,
        scratch_shapes=[pltpu.VMEM((tiles * plan.span, LANES), f32)] * 2
        + patches
        + [pltpu.SMEM((8, plan.probes), jnp.int32), pltpu.SemaphoreType.DMA],
        compiler_params=params,
        name="phases",
    )
    cos_0, sin_0, cos_1, sin_1, wave = call(
        places, top, bottom, far, near, table, known
    )
    call = pl.pallas_call(
        functools.partial(finish, plan),
        out_shape=jax.ShapeDtypeStruct((plan.pixels, plan.probes), f32),
        in_specs=[vmem] * 7,
        out_specs=vmem,
        scratch_shapes=[pltpu.VMEM((2, plan.phase_rows[0] * ROWS, LANES), f32)],
        compiler_params=params,
        name="finish",
    )
    out = call(other, wave, cos_0, sin_0, cos_1, sin_1, jnp.asarray(column_spread()))
    return out.T


def solution(mesh):
    return jax.shard_map(
        window,
        mesh=mesh,
        in_specs=(P(None, "tile", None), P("beam", None), P("beam"), P("tile"), P("tile")),
        out_specs=P("tile", "beam"),
        check_vma=False,
    )
```

```python
import functools
import math

import jax
import jax.numpy as jnp
import numpy as np
from jax import lax
from jax.experimental import pallas as pl
from jax.experimental.pallas import tpu as pltpu
from jax.sharding import PartitionSpec as P


CROP = 16
REACH = 5
LANES = 128
HALF = 64
ROWS = 8
PAD = 16
NEAR = 8
PHASE = 0.6
MIDDLE = 1.2
NUMBERS = 3


def make_taps():
    blur = [math.exp(-(j * j) / 4.5) for j in range(-REACH, REACH + 1)]
    spread = [math.exp(-(j * j) / 18.0) for j in range(-REACH, REACH + 1)]
    blur = [value / sum(blur) for value in blur]
    spread = [value / sum(spread) for value in spread]
    angles = [0.35 * j * j for j in range(-REACH, REACH + 1)]
    real = [value * math.cos(angle) for value, angle in zip(spread, angles)]
    imag = [value * math.sin(angle) for value, angle in zip(spread, angles)]
    return np.array(blur), np.array(real), np.array(imag)


def two_parts(matrix):
    high = np.asarray(matrix, np.float32).astype(jnp.bfloat16)
    low = (matrix - high.astype(np.float64)).astype(np.float32).astype(jnp.bfloat16)
    return high, low


def band(taps, count):
    matrix = np.zeros((count, count + 2 * REACH))
    for i in range(count):
        matrix[i, i : i + 2 * REACH + 1] = taps
    return matrix


def row_blur(count, stored):
    taps = np.zeros((count, stored))
    taps[:, : count + 2 * REACH] = band(make_taps()[0], count)
    full = np.einsum("rk,pq->rpqk", taps, np.eye(ROWS)).reshape(count * ROWS, ROWS * stored)
    return np.concatenate(two_parts(full), axis=0)


def column_band(taps):
    return np.kron(np.eye(2), np.pad(band(taps, HALF - 2 * REACH), ((0, 2 * REACH), (0, 0))).T)


def column_blur():
    high, low = two_parts(PHASE * column_band(make_taps()[0]))
    return np.block([[high, low], [high, np.zeros_like(low)]])


def column_spread():
    _, real, imag = make_taps()
    real, imag = column_band(real), column_band(imag)
    return np.concatenate(two_parts(np.block([[real, imag], [-imag, real]])), axis=0)


def fit(function, top, degree):
    nodes = top / 2 * (1 + np.cos(np.pi * (np.arange(200) + 0.5) / 200))
    series = np.polynomial.Chebyshev.fit(nodes, function(nodes), degree, domain=[0, top])
    return [float(c) for c in series.convert(kind=np.polynomial.Polynomial).coef]


def ROUNDS(count):
    reaches = []
    while count > 1:
        count //= 2
        reaches.append(count)
    return reaches[::-1]


def horner(coefficients, value):
    total = coefficients[-1]
    for coefficient in coefficients[-2::-1]:
        total = total * value + coefficient
    return total


def split(value):
    high = value.astype(jnp.bfloat16)
    return high, (value - high.astype(jnp.float32)).astype(jnp.bfloat16)


def product(left, right):
    return jnp.dot(left, right, preferred_element_type=jnp.float32)


def column_product(value, matrix):
    count, half = value.shape[0], matrix.shape[0] // 2
    high, low = split(value)
    both = product(jnp.concatenate([high, low], axis=0), matrix[:half])
    return both[:count] + both[count:] + product(high, matrix[half:])


def choose(plan, top_ref, bottom_ref, rows_ref, cols_ref, far_ref, near_ref, place_ref):
    find_places(plan, rows_ref, cols_ref, place_ref)
    first = lax.axis_index("beam") < lax.axis_size("beam") // 2

    @pl.when(first)
    def _():
        far_ref[...] = bottom_ref[...]
        near_ref[...] = top_ref[:, :NEAR, :]

    @pl.when(jnp.logical_not(first))
    def _():
        far_ref[...] = top_ref[...]
        near_ref[...] = bottom_ref[:, PAD - NEAR :, :]


def find_places(plan, rows_ref, cols_ref, place_ref):
    grid_cols = plan.grid_cols
    first_row, first_col = plan.origin()
    shape = place_ref.shape
    which = lax.broadcasted_iota(jnp.int32, shape, 0)
    halo = jnp.where(which < 4, plan.halo[0], plan.halo[1])
    which = which & 3
    second = (lax.broadcasted_iota(jnp.int32, shape, 1) & ROWS) * (HALF // ROWS)
    row = rows_ref[...] + (first_row + PAD - halo)
    col = cols_ref[...] + (first_col + grid_cols - halo)
    col = jnp.where(col >= grid_cols, col - grid_cols, col)
    tile, offset = lax.shift_right_logical(col, 7), col & (LANES - 1)
    beside = jnp.where(tile == grid_cols // LANES - 1, 0, tile + 1)
    place_ref[...] = jnp.where(
        which < 2,
        jnp.where(which == 0, tile, beside) * plan.span + row,
        jnp.where(which == 2, offset, (second + LANES - offset) & (LANES - 1)),
    )


def phases(
    plan,
    found_ref,
    top_ref,
    bottom_ref,
    far_ref,
    near_ref,
    table_ref,
    beam_ref,
    cos_0,
    sin_0,
    cos_1,
    sin_1,
    wave_out,
    strip_0,
    strip_1,
    patch_0,
    patch_1,
    place_ref,
    arrived,
):
    f32, bf16 = jnp.float32, jnp.bfloat16
    tiles = plan.grid_cols // LANES
    span = plan.span
    strip_rows = 2 * PAD
    strips, patches = (strip_0, strip_1), (patch_0, patch_1)
    transfer = pltpu.make_async_copy(found_ref, place_ref, arrived)
    transfer.start()
    first = lax.axis_index("beam") < lax.axis_size("beam") // 2
    far_at = jnp.where(first, 0, PAD + strip_rows)
    near_at = jnp.where(first, PAD + strip_rows, PAD - NEAR)

    for tile in range(tiles):
        lanes = slice(tile * LANES, (tile + 1) * LANES)
        at = tile * span
        for part in range(2):
            strips[part][at + PAD : at + 2 * PAD, :] = top_ref[part, :, lanes].astype(f32)
            strips[part][at + 2 * PAD : at + 3 * PAD, :] = bottom_ref[part, :, lanes].astype(f32)
            strips[part][pl.ds(at + far_at, PAD), :] = far_ref[part, :, lanes].astype(f32)
            strips[part][pl.ds(at + near_at, NEAR), :] = near_ref[part, :, lanes].astype(f32)

    wave_out[...] = common_wave(plan, beam_ref, None)
    transfer.wait()
    lane = lax.broadcasted_iota(jnp.int32, (1, LANES), 1)
    lower = jnp.where(lane < HALF, 1.0, 0.0).astype(bf16)
    upper = jnp.where(lane < HALF, 0.0, 1.0).astype(bf16)
    cos_fit = fit(lambda t: np.cos(np.sqrt(t)), MIDDLE**2, 4)
    sin_fit = fit(lambda t: np.sinc(np.sqrt(t) / np.pi), MIDDLE**2, 3)
    outs = ((cos_0, sin_0), (cos_1, sin_1))
    tables = []
    at = 0
    for shape in plan.tables:
        tables.append(table_ref[at : at + shape[0], : shape[1]])
        at += shape[0]
    for part in (1, 0):
        strip, patch, stored = strips[part], patches[part], plan.stored[part]

        def window(probe):
            here, there, offset, shift = [place_ref[4 * part + i, probe] for i in range(4)]
            both = jnp.where(
                lane >= offset, strip[pl.ds(here, stored), :], strip[pl.ds(there, stored), :]
            )
            return pltpu.roll(both, shift, 1)

        for pair in range(plan.probes // 2):
            probe = pair // ROWS * 2 * ROWS + pair % ROWS
            both = lower * window(probe).astype(bf16) + upper * window(probe + ROWS).astype(bf16)
            patch[pair * stored : (pair + 1) * stored, :] = both.astype(patch.dtype)

        count = ROWS * stored
        size = plan.phase_rows[part] * ROWS
        for group in range(0, plan.groups, 2):
            counts = [patch[g * count : (g + 1) * count] for g in (group, group + 1)]
            counts = jnp.concatenate([value.astype(bf16) for value in counts], axis=1)
            both = product(tables[part], counts)
            both = both[:size] + both[size:]
            along = jnp.concatenate([both[:, :LANES], both[:, LANES:]], axis=0)
            phase = product(jnp.concatenate(split(along), axis=1), tables[2])
            phase = phase[:, :LANES] + (phase[:, LANES:] - MIDDLE)
            square = phase * phase
            cos_out, sin_out = outs[part]
            cos_out[group * size : (group + 2) * size] = horner(cos_fit, square)
            sin_out[group * size : (group + 2) * size] = phase * horner(sin_fit, square)


def common_wave(plan, beam_ref, total):
    f32 = jnp.float32
    turn_fit = fit(lambda t: 2 * np.pi * np.sinc(2 * np.sqrt(t)), 0.0625, 5)
    first_row, first_col = plan.origin()
    shape = plan.wave_shape
    dx = lax.broadcasted_iota(jnp.int32, shape, 0) + (first_row - 2 * REACH)
    lane = lax.broadcasted_iota(jnp.int32, shape, 1)
    dy = (lane & (HALF - 1)) + (first_col - 2 * REACH)
    dx = dx.astype(f32) * (1.0 / plan.grid_rows)
    dy = dy.astype(f32) * (1.0 / plan.grid_cols)
    quarter = jnp.where(lane >= HALF, 0.25, 0.0).astype(f32)
    beams = beam_ref.shape[0]
    numbers = [jnp.broadcast_to(beam_ref[:, i : i + 1], (beams, LANES)) for i in range(NUMBERS)]
    for beam in range(beams):
        row, col, weight = [number[beam : beam + 1] for number in numbers]
        turns = row * dx + (col * dy - quarter)
        left = 0.25 - jnp.abs(turns - jnp.round(turns))
        term = (weight * left) * horner(turn_fit, left * left)
        total = term if total is None else total + term
    return total


def expand_wave(both, wave_ref):
    upper = lax.broadcasted_iota(jnp.int32, both.shape, 1) >= HALF
    turned = pltpu.roll(both, HALF, 1)
    real = jnp.where(upper, turned, both)
    imag = jnp.where(upper, both, turned)
    for r in range(wave_ref.shape[1] // ROWS):
        at = slice(r * ROWS, (r + 1) * ROWS)
        wave_ref[0, at, :] = jnp.broadcast_to(real[r : r + 1], (ROWS, LANES))
        wave_ref[1, at, :] = jnp.broadcast_to(imag[r : r + 1], (ROWS, LANES))


def spread_rows(wave, count):
    _, real_taps, imag_taps = make_taps()
    half = wave.shape[0] // 2
    out = []
    for at in range(count):
        sums = []
        for base in (0, half):
            rows = [
                wave[base + (at + j) * ROWS : base + (at + j + 1) * ROWS] for j in range(2 * REACH + 1)
            ]
            pairs = [rows[REACH]] + [rows[REACH - j] + rows[REACH + j] for j in range(1, REACH + 1)]
            sums.append(
                [
                    sum(float(taps[REACH + j]) * pairs[j] for j in range(start, REACH + 1))
                    for taps, start in ((real_taps, 0), (imag_taps, 1))
                ]
            )
        (real_real, real_imag), (imag_real, imag_imag) = sums
        out.append(jnp.concatenate([real_real - imag_imag, imag_real + real_imag], axis=1))
    return jnp.concatenate(out, axis=0)


def turn(real, imag, cos, sin):
    return jnp.concatenate([real * cos - imag * sin, real * sin + imag * cos], axis=0)


class Plan:
    def __init__(self, grid_rows, grid_cols, beams, probes, pixels, span):
        self.grid_rows, self.grid_cols = grid_rows, grid_cols
        self.beams, self.probes, self.pixels = beams, probes, pixels
        self.groups = probes // (2 * ROWS)
        self.take_cols = min(pixels, CROP)
        self.take_rows = pixels // self.take_cols
        self.halo = [3 * REACH, 2 * REACH]
        self.span = span
        self.wave_shape = (-(-(self.take_rows + 4 * REACH) // ROWS) * ROWS, LANES)
        self.phase_rows = [self.take_rows + 4 * REACH, self.take_rows + 2 * REACH]
        self.stored = [-(-(count + 2 * REACH) // ROWS) * ROWS for count in self.phase_rows]

    def origin(self):
        first = lax.axis_index("beam").astype(jnp.int32) * self.pixels
        return first // CROP, first % CROP


def finish(
    plan,
    beam_ref,
    half_wave,
    cos_0,
    sin_0,
    cos_1,
    sin_1,
    spread_cols,
    out_ref,
    start,
):
    expand_wave(common_wave(plan, beam_ref, half_wave[...]), start)
    parts = [range(first, first + 1) for first in range(0, plan.groups, 1)]
    middles = []
    for part in parts:
        count = plan.phase_rows[0] * ROWS
        rows = []
        for group in part:
            at = slice(group * count, (group + 1) * count)
            wave = turn(start[0], start[1], cos_0[at], sin_0[at])
            rows.append(spread_rows(wave, plan.phase_rows[1]))
        middles.append(column_product(jnp.concatenate(rows, axis=0), spread_cols[...]))
    finals = []
    for part, middle in zip(parts, middles):
        count = plan.phase_rows[1] * ROWS
        rows = []
        for group in part:
            at = slice(group * count, (group + 1) * count)
            here = slice((group - part[0]) * count, (group - part[0] + 1) * count)
            wave = turn(middle[here, :LANES], middle[here, LANES:], cos_1[at], sin_1[at])
            rows.append(spread_rows(wave, plan.take_rows))
        finals += rows
    wave = column_product(jnp.concatenate(finals, axis=0), spread_cols[...])
    lane = lax.broadcasted_iota(jnp.int32, (ROWS, LANES), 1)
    blocks = []
    count = plan.take_rows * ROWS
    for group in range(plan.groups):
        final = wave[group * count : (group + 1) * count]
        real, imag = final[:, :LANES], final[:, LANES:]
        power = (real * real + imag * imag) * (1.0 / plan.beams)
        for place in (0, HALF):
            block = None
            for r in range(plan.take_rows):
                moved = power[r * ROWS : (r + 1) * ROWS]
                shift = (r * plan.take_cols - place) % LANES
                moved = pltpu.roll(moved, shift, 1) if shift else moved
                block = moved if r == 0 else jnp.where(lane < r * plan.take_cols, block, moved)
            blocks.append(block)
    out_ref[...] = jnp.concatenate(blocks, axis=0).T[: plan.pixels]


def window(atom_counts, beam_index, beam_weight, probe_rows, probe_cols):
    slices, strip_rows, grid_cols = atom_counts.shape
    beam_parts, tile_parts = lax.axis_size("beam"), lax.axis_size("tile")
    plan = Plan(
        strip_rows * tile_parts,
        grid_cols,
        beam_weight.shape[0] * beam_parts,
        probe_rows.shape[0],
        CROP * CROP // beam_parts,
        strip_rows + 2 * PAD + 1,
    )

    f32, bf16 = jnp.float32, jnp.bfloat16
    vmem = pl.BlockSpec(memory_space=pltpu.VMEM)
    smem = pl.BlockSpec(memory_space=pltpu.SMEM)
    params = pltpu.CompilerParams(vmem_limit_bytes=12 << 20)
    tiles = grid_cols // LANES
    known = jnp.concatenate([beam_index.astype(f32), beam_weight[:, None]], axis=1)
    known = jnp.pad(known, ((0, 0), (0, LANES - NUMBERS)))

    top, bottom = atom_counts[:, :PAD], atom_counts[:, strip_rows - PAD :]
    tables = [row_blur(plan.phase_rows[part], plan.stored[part]) for part in range(2)]
    tables.append(column_blur())
    plan.tables = [table.shape for table in tables]
    width = max(cols for _, cols in plan.tables)
    table = np.concatenate([np.pad(t, ((0, 0), (0, width - t.shape[1]))) for t in tables])
    table = jnp.asarray(table)
    far, near, places = pl.pallas_call(
        functools.partial(choose, plan),
        out_shape=[
            jax.ShapeDtypeStruct((slices, PAD, grid_cols), bf16),
            jax.ShapeDtypeStruct((slices, NEAR, grid_cols), bf16),
            jax.ShapeDtypeStruct((8, plan.probes), jnp.int32),
        ],
        in_specs=[vmem] * 4,
        out_specs=[vmem] * 3,
        compiler_params=pltpu.CompilerParams(vmem_limit_bytes=2 << 20),
        name="choose",
    )(top, bottom, probe_rows[None], probe_cols[None])

    def pass_on(rows, step):
        pairs = []
        for beam in range(beam_parts):
            move = step if beam < beam_parts // 2 else -step
            for tile in range(tile_parts):
                pairs.append((beam * tile_parts + tile, beam * tile_parts + (tile + move) % tile_parts))
        return lax.ppermute(rows, ("beam", "tile"), pairs)

    far = pass_on(far, 1)
    near = pass_on(near, -1)
    other = None
    for reach in ROUNDS(beam_parts):
        if other is not None:
            known = jnp.concatenate([known, other], axis=0)
        other = lax.ppermute(known, "beam", [(i, i ^ reach) for i in range(beam_parts)])

    shapes = [(plan.groups * count * ROWS, LANES) for count in plan.phase_rows]
    shapes = [jax.ShapeDtypeStruct(shape, f32) for shape in shapes]
    patches = []
    for stored in plan.stored:
        kind = bf16 if stored % (2 * ROWS) == 0 else f32
        patches.append(pltpu.VMEM((plan.probes // 2 * stored, LANES), kind))
    call = pl.pallas_call(
        functools.partial(phases, plan),
        out_shape=[shapes[0]] * 2 + [shapes[1]] * 2 + [jax.ShapeDtypeStruct(plan.wave_shape, f32)],
        in_specs=[vmem] * 7,
        out_specs=[vmem] * 5,
        scratch_shapes=[pltpu.VMEM((tiles * plan.span, LANES), f32)] * 2
        + patches
        + [pltpu.SMEM((8, plan.probes), jnp.int32), pltpu.SemaphoreType.DMA],
        compiler_params=params,
        name="phases",
    )
    cos_0, sin_0, cos_1, sin_1, wave = call(
        places, top, bottom, far, near, table, known
    )
    call = pl.pallas_call(
        functools.partial(finish, plan),
        out_shape=jax.ShapeDtypeStruct((plan.pixels, plan.probes), f32),
        in_specs=[vmem] * 7,
        out_specs=vmem,
        scratch_shapes=[pltpu.VMEM((2, plan.phase_rows[0] * ROWS, LANES), f32)],
        compiler_params=params,
        name="finish",
    )
    out = call(other, wave, cos_0, sin_0, cos_1, sin_1, jnp.asarray(column_spread()))
    return out.T


def solution(mesh):
    return jax.shard_map(
        window,
        mesh=mesh,
        in_specs=(P(None, "tile", None), P("beam", None), P("beam"), P("tile"), P("tile")),
        out_specs=P("tile", "beam"),
        check_vma=False,
    )
```
